128 devices in a mesh: grp: 8 (over y, core), dev: 16 (over x, z).
Axes of the slice: x: 4, y: 4, z: 4, core: 2. Of those that a mesh axis runs over, the one named last changes fastest.
Arguments:
- suffix_queries: bfloat16 [16384, 2048], P(('grp', 'dev')), may hold values from -12 to 12
- suffix_keys: bfloat16 [16384, 2048], P(('grp', 'dev')), may hold values from -12 to 12
- suffix_values: bfloat16 [16384, 2048], P(('grp', 'dev')), may hold values from -6 to 6
- layer_input: bfloat16 [16384, 2048], P(('grp', 'dev')), may hold values from -6 to 6
- suffix_lengths: int32 [128, 8], P(('grp', 'dev')), may hold values from 1 to 32, as said below
- request_group: int32 [128, 8], P(('grp', 'dev')), may hold values from 0 to 7, as said below
- prefix_keys: bfloat16 [8, 4096, 2048], P('grp', None, 'dev'), may hold values from -12 to 12
- prefix_values: bfloat16 [8, 4096, 2048], P('grp', None, 'dev'), may hold values from -6 to 6
- up_weight: bfloat16 [2048, 8192], P(None, ('grp', 'dev')), may hold values from -0.125 to 0.125
- up_bias: bfloat16 [8192], P(('grp', 'dev')), may hold values from -3 to 3
- down_weight: bfloat16 [8192, 2048], P(('grp', 'dev')), may hold values from -0.0625 to 0.0625
- down_bias: float32 [2048], replicated, may hold values from -3 to 3
- attn_gain: float32 [2048], replicated, may hold values from 0.5 to 1.5
- attn_shift: float32 [2048], replicated, may hold values from -2 to 2
- out_gain: float32 [2048], replicated, may hold values from 0.5 to 1.5
- out_shift: float32 [2048], replicated, may hold values from -2 to 2
Outputs:
- layer_output: bfloat16 [16384, 2048], P(('grp', 'dev'))
The draws below stay inside these ranges and needn't reach their ends.
Inputs may be any that keep to these rules, and one draw needn't show every extreme that they name: `suffix_lengths`: each row lists one device's 8 requests in slot order; they fill its 128 slots exactly, and at least one of them has 32 tokens. `request_group`: the 8 requests of one row name every prefix exactly once.
All inputs are finite; a program needn't handle non-finite values.
Results may differ from the reference program's by a relative error of at most 0.014.
Values may be sent and summed in bfloat16 or wider, within the bound.
A program may use at most 128 MiB of HBM per device.

```python
import jax
import jax.numpy as jnp
from jax import lax

D = 2048
HEADS = 16
HD = 128
FF = 8192
PLEN = 4096
TOK_DEV = 128
PREFIXES = 8
REQ_DEV = 8
MOST = 32
TOKENS = 16384
N_GRP = 8
N_DEV = 16


def draw_suffix_queries(key, part):
    drawn_draw = 1.5 * jax.random.truncated_normal(jax.random.fold_in(key, 11), -5.0, 5.0, (TOKENS, D), jnp.float32)
    return drawn_draw.astype(jnp.bfloat16)


def draw_suffix_keys(key, part):
    drawn_draw = 1.5 * jax.random.truncated_normal(jax.random.fold_in(key, 17), -5.0, 5.0, (TOKENS, D), jnp.float32)
    return drawn_draw.astype(jnp.bfloat16)


def draw_prefix_keys(key, part):
    drawn_draw = 1.5 * jax.random.truncated_normal(jax.random.fold_in(key, 13), -5.0, 5.0, (PREFIXES, PLEN, D), jnp.float32)
    return drawn_draw.astype(jnp.bfloat16)


def draw_suffix_lengths(key, part):
    row_total = TOKENS // TOK_DEV
    others = REQ_DEV - 1
    extra_total = TOK_DEV - MOST - others

    def one_device(device_key):
        weight_key, step_key, order_key = jax.random.split(device_key, 3)
        weights = jax.random.randint(weight_key, (others,), 1, 9).astype(jnp.int32)
        labels = lax.iota(jnp.int32, others)

        def add_unit(step, filled):
            score_draw = jax.random.randint(jax.random.fold_in(step_key, step), (others,), 0, 1024).astype(jnp.int32)
            score = score_draw * weights * REQ_DEV + labels
            score = jnp.where(filled < MOST, score, -1)
            pick = jnp.argmax(score).astype(jnp.int32)
            return (filled + (labels == pick).astype(jnp.int32)).astype(jnp.int32)
        filled = lax.fori_loop(0, extra_total, add_unit, jnp.ones((others,), jnp.int32))
        pieces = jnp.concatenate([jnp.full((1,), MOST, jnp.int32), filled]).astype(jnp.int32)
        return jnp.take(pieces, jax.random.permutation(order_key, REQ_DEV)).astype(jnp.int32)
    return jax.vmap(one_device)(jax.random.split(key, row_total))


def draw_request_group(key, part):
    row_total = TOKENS // TOK_DEV

    def one_device(device_key):
        return jax.random.permutation(device_key, PREFIXES)[:REQ_DEV].astype(jnp.int32)
    return jax.vmap(one_device)(jax.random.split(key, row_total))


def block_scale(own_key, shape, cuts, least, top_value):
    level, own = 1.0, jax.random.fold_in(own_key, 6)
    for axis_at, shards_of in cuts:
        heights = jnp.exp(jax.random.uniform(jax.random.fold_in(own, axis_at), (shards_of,), jnp.float32, least / len(cuts), top_value / len(cuts)))
        level = level * jnp.repeat(heights, shape[axis_at] // shards_of).reshape([-1 if axis == axis_at else 1 for axis in range(len(shape))])
    return level


def bell_draw(stream_key, shape, deviation, bound, shards=(), held_as=jnp.bfloat16):
    array = jax.random.normal(stream_key, shape, jnp.float32) * deviation
    if len(shards) > 0:
        array = block_scale(stream_key, shape, shards, -0.22, 0.18) * array
    return jnp.clip(array, min=-bound, max=bound).astype(held_as)


def setup_inputs(seed: int = 0) -> dict:
    arg_keys = jax.random.split(jax.random.key(seed), 17)
    suffix_queries = draw_suffix_queries(jax.random.fold_in(arg_keys[16], 71), 0)
    suffix_keys = draw_suffix_keys(jax.random.fold_in(arg_keys[16], 71), 0)
    suffix_values = bell_draw(arg_keys[2], (TOKENS, D), 1.0, 6.0, ((0, 128),))
    layer_input = bell_draw(arg_keys[3], (TOKENS, D), 1.0, 6.0, ((0, 128),))
    suffix_lengths = draw_suffix_lengths(jax.random.fold_in(arg_keys[16], 71), 0)
    request_group = draw_request_group(jax.random.fold_in(arg_keys[16], 71), 0)
    prefix_keys = draw_prefix_keys(jax.random.fold_in(arg_keys[16], 71), 0)
    prefix_values = bell_draw(arg_keys[7], (PREFIXES, PLEN, D), 1.0, 6.0, ((0, 8), (2, 16)))
    up_weight = bell_draw(arg_keys[8], (D, FF), D ** -0.5, 0.125, ((1, 128),))
    up_bias = bell_draw(arg_keys[9], (FF,), 0.5, 3.0, ((0, 128),))
    down_weight = bell_draw(arg_keys[10], (FF, D), FF ** -0.5, 0.0625, ((0, 128),))
    down_bias = bell_draw(arg_keys[11], (D,), 0.5, 3.0, (), jnp.float32)
    attn_gain = jnp.clip(1.0 + 0.1 * jax.random.normal(arg_keys[12], (D,), jnp.float32), 0.5, 1.5)
    attn_shift = bell_draw(arg_keys[13], (D,), 0.3, 2.0, (), jnp.float32)
    out_gain = jnp.clip(1.0 + 0.1 * jax.random.normal(arg_keys[14], (D,), jnp.float32), 0.5, 1.5)
    out_shift = bell_draw(arg_keys[15], (D,), 0.3, 2.0, (), jnp.float32)
    return {"suffix_queries": suffix_queries, "suffix_keys": suffix_keys, "suffix_values": suffix_values, "layer_input": layer_input, "suffix_lengths": suffix_lengths, "request_group": request_group, "prefix_keys": prefix_keys, "prefix_values": prefix_values, "up_weight": up_weight, "up_bias": up_bias, "down_weight": down_weight, "down_bias": down_bias, "attn_gain": attn_gain, "attn_shift": attn_shift, "out_gain": out_gain, "out_shift": out_shift}


norm_eps = 1e-12

def layer_norm(summed, norm_gain, norm_shift):
    row_mean = lax.optimization_barrier(jnp.mean(summed, axis=-1, keepdims=True))
    centred = summed - row_mean
    spread = lax.optimization_barrier(jnp.mean(centred * centred, axis=-1, keepdims=True))
    return centred * lax.rsqrt(spread + norm_eps) * norm_gain + norm_shift

def request_layout(lengths, slot_count):
    lengths = lengths.astype(jnp.int32)
    end_points = jnp.cumsum(lengths).astype(jnp.int32)
    starts = (end_points - lengths).astype(jnp.int32)
    positions = lax.iota(jnp.int32, slot_count)
    member = (positions[:, None] >= starts[None, :]) & (positions[:, None] < end_points[None, :])
    slot_ids = lax.iota(jnp.int32, lengths.shape[0])
    segment = lax.optimization_barrier(jnp.sum(jnp.where(member, slot_ids[None, :], 0), axis=1)).astype(jnp.int32)
    return (starts, segment)

def attend_suffix(query_rows, key_rows, value_rows, segment):
    slot_count = query_rows.shape[0]
    query_heads = query_rows.astype(jnp.float32).reshape(slot_count, HEADS, HD)
    key_heads = key_rows.astype(jnp.float32).reshape(slot_count, HEADS, HD)
    value_heads = value_rows.astype(jnp.float32).reshape(slot_count, HEADS, HD)
    scores = jnp.einsum('qhd,khd->hqk', query_heads, key_heads) * HD ** (-0.5)
    positions = lax.iota(jnp.int32, slot_count)
    visible = ((segment[:, None] == segment[None, :]) & (positions[None, :] <= positions[:, None]))[None]
    row_top = lax.optimization_barrier(jnp.max(jnp.where(visible, scores, -jnp.inf), axis=2))
    weights = jnp.where(visible, jnp.exp(scores - row_top[:, :, None]), 0.0)
    row_sum = lax.optimization_barrier(jnp.sum(weights, axis=2))
    rounded = lax.optimization_barrier(weights.astype(jnp.bfloat16)).astype(jnp.float32)
    mixed_sum = jnp.einsum('hqk,khd->qhd', rounded, value_heads)
    return (row_top.T, row_sum.T, mixed_sum)

def merge_parts(far_answer, far_top, far_sum, own_top, own_sum, own_mixed):
    far_top = far_top.astype(jnp.float32)
    far_sum = far_sum.astype(jnp.float32)
    joint_top = jnp.maximum(far_top, own_top)
    far_weight = jnp.exp(far_top - joint_top) * far_sum
    own_weight = jnp.exp(own_top - joint_top)
    numerator = far_weight[:, :, None] * far_answer.astype(jnp.float32) + own_weight[:, :, None] * own_mixed
    return numerator / (far_weight + own_weight * own_sum)[:, :, None]

def reference(suffix_queries, suffix_keys, suffix_values, layer_input, suffix_lengths, request_group, prefix_keys, prefix_values, up_weight, up_bias, down_weight, down_bias, attn_gain, attn_shift, out_gain, out_shift):
    device_total = N_GRP * N_DEV
    anchor = jnp.zeros((), jnp.int32)

    def per_device(stacked):
        query_rows, key_rows, value_rows, input_rows, lengths, groups = stacked
        lengths = lengths.astype(jnp.int32)
        groups = groups.astype(jnp.int32)
        starts, segment = request_layout(lengths, TOK_DEV)
        padded = jnp.concatenate([query_rows, jnp.zeros((MOST, D), query_rows.dtype)], axis=0)
        placed_answer = jnp.zeros((TOK_DEV + MOST, D), jnp.bfloat16)
        placed_top = jnp.zeros((TOK_DEV + MOST, HEADS), jnp.bfloat16)
        placed_sum = jnp.zeros((TOK_DEV + MOST, HEADS), jnp.bfloat16)
        for request in range(REQ_DEV):
            taken = lax.dynamic_slice_in_dim(padded, starts[request], MOST, 0).astype(jnp.float32).reshape(MOST, HEADS, HD)
            cache_keys = lax.dynamic_index_in_dim(prefix_keys, groups[request], 0, keepdims=False).astype(jnp.float32).reshape(PLEN, HEADS, HD)
            cache_values = lax.dynamic_index_in_dim(prefix_values, groups[request], 0, keepdims=False).astype(jnp.float32).reshape(PLEN, HEADS, HD)
            scores = jnp.einsum('qhd,khd->hqk', taken, cache_keys) * HD ** (-0.5)
            row_top = lax.optimization_barrier(jnp.max(scores, axis=2)).astype(jnp.bfloat16)
            weights = jnp.exp(scores - lax.optimization_barrier(row_top).astype(jnp.float32)[:, :, None])
            row_sum = lax.optimization_barrier(jnp.sum(weights, axis=2))
            rounded = lax.optimization_barrier(weights.astype(jnp.bfloat16)).astype(jnp.float32)
            mixed_sum = jnp.einsum('hqk,khd->qhd', rounded, cache_values)
            answer = (mixed_sum / row_sum.T[:, :, None]).astype(jnp.bfloat16).reshape(MOST, D)
            placed_answer = lax.dynamic_update_slice(placed_answer, answer, (starts[request], anchor))
            placed_top = lax.dynamic_update_slice(placed_top, row_top.T, (starts[request], anchor))
            placed_sum = lax.dynamic_update_slice(placed_sum, row_sum.T.astype(jnp.bfloat16), (starts[request], anchor))
        own_top, own_sum, own_mixed = attend_suffix(query_rows, key_rows, value_rows, segment)
        far_answer = placed_answer[:TOK_DEV].reshape(TOK_DEV, HEADS, HD)
        context = merge_parts(far_answer, placed_top[:TOK_DEV], placed_sum[:TOK_DEV], own_top, own_sum, own_mixed)
        hidden_state = layer_norm(input_rows.astype(jnp.float32) + context.reshape(TOK_DEV, D), attn_gain, attn_shift).astype(jnp.bfloat16)
        product = jnp.dot(hidden_state, up_weight, preferred_element_type=jnp.float32)
        activation = jax.nn.gelu(product + up_bias.astype(jnp.float32), approximate=True).astype(jnp.bfloat16)
        mlp_sum = jnp.dot(activation, down_weight, preferred_element_type=jnp.float32)
        return layer_norm(hidden_state.astype(jnp.float32) + mlp_sum + down_bias, out_gain, out_shift).astype(jnp.bfloat16)
    stacked = (suffix_queries.reshape(device_total, TOK_DEV, D), suffix_keys.reshape(device_total, TOK_DEV, D), suffix_values.reshape(device_total, TOK_DEV, D), layer_input.reshape(device_total, TOK_DEV, D), suffix_lengths, request_group)
    outputs = lax.map(per_device, stacked)
    return outputs.reshape(TOKENS, D)
```

```python
import functools

import jax
import jax.numpy as jnp
from jax import lax
from jax.experimental import pallas as pl
from jax.experimental.pallas import tpu as pltpu
from jax.sharding import Mesh, PartitionSpec as P

HD = 128
NY, NC, NX, NZ = 4, 2, 4, 4
GRP, DEV = NY * NC, NX * NZ
CAP = 32
LOG2E = 1.4426950408889634
SCALE2 = HD**-0.5 * LOG2E
NORM_EPS = 1e-12
NEG = -1e30
MESH = pl.DeviceIdType.MESH
NT_DIMS = (((1,), (1,)), ((), ()))
LIMIT = 64 * 1024 * 1024 - 65536


def coordinates():
    return tuple(lax.axis_index(name) for name in ("y", "c", "x", "z"))


def place(y, c, x, z):
    return {"y": y, "c": c, "x": x, "z": z}


def plane_at(x, z, block):
    return lax.rem(x + block // NZ, NX), lax.rem(z + lax.rem(block, NZ), NZ)


def plane_back(x, z, block):
    return lax.rem(x + NX - block // NZ, NX), lax.rem(z + NZ - lax.rem(block, NZ), NZ)


def wait_bytes(ref, sem):
    pltpu.make_async_copy(ref, ref, sem).wait()


def norm_rows(summed, gain, shift):
    mean = jnp.mean(summed, axis=-1, keepdims=True)
    centred = summed - mean
    spread = jnp.mean(centred * centred, axis=-1, keepdims=True)
    return centred * lax.rsqrt(spread + NORM_EPS) * gain + shift


def slot_tables(len_ref, grp_ref, shape, dim):
    slot = lax.broadcasted_iota(jnp.int32, shape, dim)
    start = jnp.int32(0)
    group = jnp.zeros(shape, jnp.int32)
    rank = jnp.zeros(shape, jnp.int32)
    for request in range(len_ref.shape[1]):
        length = len_ref[0, request]
        inside = (slot >= start) & (slot < start + length)
        group = jnp.where(inside, grp_ref[0, request], group)
        rank = jnp.where(inside, slot - start, rank)
        start = start + length
    return group, rank


def prefix_kernel(
    len_ref, grp_ref, q_ref, k_ref, v_ref, x_ref, bias_ref, pk_ref, pv_ref, gain_ref, shift_ref,
    hid_ref, bias_out,
    qs, qr, ans_s, ans_r, lse_s, lse_r, bias_r, s0, s1, p0, p1, acc, lcol, lsecol, mixed, own_top, own_sum,
    q_send, q_recv, a_send, a_recv, l_send, l_recv, b_send, b_recv, self_sem,
):
    y, c, x, z = coordinates()
    me_g = y * NC + c
    me_d = x * NZ + z
    slots = q_ref.shape[0]
    heads = q_ref.shape[1] // HD
    s_bufs, p_bufs = (s0, s1), (p0, p1)
    rows = GRP * CAP
    plen = pk_ref.shape[0]

    def group_at(k):
        g = lax.rem(me_g + k, GRP)
        return g, g // NC, lax.rem(g, NC)

    barrier = pltpu.get_barrier_semaphore()

    def greet(block, k):
        tx, tz = plane_at(x, z, block)
        _, ty, tc = group_at(k)
        pl.semaphore_signal(barrier, inc=1, device_id=place(ty, tc, tx, tz), device_id_type=MESH)

    for k in range(1, GRP):
        greet(0, k)

    @pl.loop(1, DEV)
    def _(block):
        for k in range(GRP):
            greet(block, k)

    group_row, rank_row = slot_tables(len_ref, grp_ref, (1, slots), 1)
    pick = lax.broadcasted_iota(jnp.int32, (rows, slots), 0) == group_row * CAP + rank_row
    pick = pick.astype(jnp.float32).astype(jnp.bfloat16)
    for d in range(heads):
        packed = jnp.dot(pick, q_ref[:, d * HD : (d + 1) * HD], preferred_element_type=jnp.float32)
        packed = packed.astype(jnp.bfloat16).reshape(GRP, CAP, HD)
        for g in range(GRP):
            qs[g * DEV + d] = packed[g]
    pl.semaphore_wait(barrier, GRP * DEV - 1)

    def send_query(block, k):
        tx, tz = plane_at(x, z, block)
        g, ty, tc = group_at(k)
        pltpu.make_async_remote_copy(
            src_ref=qs.at[g * DEV + tx * NZ + tz],
            dst_ref=qr.at[block * GRP + me_g],
            send_sem=q_send,
            recv_sem=q_recv.at[block],
            device_id=place(ty, tc, tx, tz),
            device_id_type=MESH,
        ).start()

    own_query = pltpu.make_async_copy(qs.at[me_g * DEV + me_d], qr.at[me_g], self_sem.at[0])
    own_query.start()
    for k in range(1, GRP):
        send_query(0, k)

    @pl.loop(1, DEV)
    def _(block):
        for k in range(GRP):
            send_query(block, k)

    for k in range(1, NC * DEV):
        tc = lax.rem(c + k // DEV, NC)
        tx, tz = plane_at(x, z, k % DEV)
        pltpu.make_async_remote_copy(
            src_ref=bias_ref,
            dst_ref=bias_r.at[c * DEV + me_d],
            send_sem=b_send,
            recv_sem=b_recv,
            device_id=place(y, tc, tx, tz),
            device_id_type=MESH,
        ).start()
    own_bias = pltpu.make_async_copy(bias_ref, bias_r.at[c * DEV + me_d], self_sem.at[3])
    own_bias.start()

    group_col, rank_col = slot_tables(len_ref, grp_ref, (slots, 1), 0)
    visible = (group_col == group_row) & (
        lax.broadcasted_iota(jnp.int32, (slots, slots), 1)
        <= lax.broadcasted_iota(jnp.int32, (slots, slots), 0)
    )

    @pl.loop(0, heads)
    def _(h):
        cols = pl.ds(pl.multiple_of(h * HD, HD), HD)
        s = lax.dot_general(q_ref[:, cols], k_ref[:, cols], NT_DIMS, preferred_element_type=jnp.float32)
        s = jnp.where(visible, s * SCALE2, NEG)
        top = jnp.max(s, axis=1, keepdims=True)
        w = jnp.where(visible, jnp.exp2(s - top), 0.0)
        own_top[h] = top
        own_sum[h] = jnp.sum(w, axis=1, keepdims=True)
        mixed[:, cols] = jnp.dot(w.astype(jnp.bfloat16), v_ref[:, cols], preferred_element_type=jnp.float32)

    def answer_back(block, k):
        tx, tz = plane_back(x, z, block)
        g, ty, tc = group_at(k)
        where = place(ty, tc, tx, tz)
        pltpu.make_async_remote_copy(
            src_ref=ans_s.at[block * GRP + g],
            dst_ref=ans_r.at[me_d * GRP + me_g],
            send_sem=a_send, recv_sem=a_recv, device_id=where, device_id_type=MESH,
        ).start()
        pltpu.make_async_remote_copy(
            src_ref=lse_s.at[block * GRP + g],
            dst_ref=lse_r.at[me_d * GRP + me_g],
            send_sem=l_send, recv_sem=l_recv, device_id=where, device_id_type=MESH,
        ).start()

    steps = 8
    span = plen // steps
    part = rows // steps

    def stage(i, parity, scoring, weighing, mixing, first=False):
        other = 1 - parity
        if scoring:
            if first:
                wait_bytes(qr.at[pl.ds(0, GRP - 1)], q_recv.at[0])
                own_query.wait()
            else:
                wait_bytes(qr.at[pl.ds(i * GRP, GRP)], q_recv.at[i])
        if mixing:
            acc[...] = jnp.zeros_like(acc)

        @pl.loop(0, steps)
        def _(j):
            keys = pl.ds(pl.multiple_of(j * span, span), span)
            if scoring:
                block = qr[pl.ds(i * GRP, GRP)].reshape(rows, HD)
                s_bufs[parity][:, keys] = lax.dot_general(
                    block, pk_ref[keys, :], NT_DIMS, preferred_element_type=jnp.float32
                )
            if weighing:
                some = pl.ds(pl.multiple_of(j * part, part), part)
                s = s_bufs[other][some, :]
                top = jnp.max(s, axis=1, keepdims=True) * SCALE2
                w = jnp.exp2(s * SCALE2 - top)
                total = jnp.sum(w, axis=1, keepdims=True)
                p_bufs[other][some, :] = w.astype(jnp.bfloat16)
                lcol[other, some, :] = total
                lsecol[other, some, :] = top + jnp.log(total) * LOG2E
            if mixing:
                acc[...] += jnp.dot(p_bufs[parity][:, keys], pv_ref[keys, :], preferred_element_type=jnp.float32)

        if mixing:
            done = i - 2
            answer = (acc[...] / lcol[parity]).astype(jnp.bfloat16).reshape(GRP, CAP, HD)
            spread = jnp.broadcast_to(lsecol[parity], (rows, HD)).reshape(GRP, CAP, HD)
            diagonal = lax.broadcasted_iota(jnp.int32, (GRP, CAP, HD), 1) == lax.broadcasted_iota(
                jnp.int32, (GRP, CAP, HD), 2
            )
            lines = jnp.sum(jnp.where(diagonal, spread, 0.0), axis=1)
            for g in range(GRP):
                ans_s[done * GRP + g] = answer[g]
                lse_s[done * GRP + g] = lines[g : g + 1]

    def send_back(done):
        for k in range(GRP):
            answer_back(done, k)

    stage(0, 0, True, False, False, first=True)
    stage(1, 1, True, True, False)
    stage(2, 0, True, True, True)
    own_answer = pltpu.make_async_copy(ans_s.at[me_g], ans_r.at[me_d * GRP + me_g], self_sem.at[1])
    own_lse = pltpu.make_async_copy(lse_s.at[me_g], lse_r.at[me_d * GRP + me_g], self_sem.at[2])
    own_answer.start()
    own_lse.start()
    for k in range(1, GRP):
        answer_back(0, k)
    stage(3, 1, True, True, True)
    send_back(1)

    @pl.loop(2, DEV // 2)
    def _(pair):
        stage(2 * pair, 0, True, True, True)
        send_back(2 * pair - 2)
        stage(2 * pair + 1, 1, True, True, True)
        send_back(2 * pair - 1)

    stage(DEV, 0, False, True, True)
    send_back(DEV - 2)
    stage(DEV + 1, 1, False, False, True)
    send_back(DEV - 1)

    own_bias.wait()
    wait_bytes(bias_r.at[pl.ds(0, NC * DEV - 1)], b_recv)
    for half in range(NC):
        for e in range(DEV // 2):
            at = half * DEV + 2 * e
            bias_out[half : half + 1, e * HD : (e + 1) * HD] = bias_r[at] + bias_r[at + 1]

    own_answer.wait()
    own_lse.wait()
    wait_bytes(ans_r.at[pl.ds(0, GRP * DEV - 1)], a_recv)
    wait_bytes(lse_r.at[pl.ds(0, GRP * DEV - 1)], l_recv)
    unpick = lax.broadcasted_iota(jnp.int32, (slots, rows), 1) == group_col * CAP + rank_col
    unpick = unpick.astype(jnp.float32).astype(jnp.bfloat16)
    lane = lax.broadcasted_iota(jnp.int32, (slots, HD), 1)

    @pl.loop(0, heads)
    def _(h):
        cols = pl.ds(pl.multiple_of(h * HD, HD), HD)
        far = jnp.dot(
            unpick, ans_r[pl.ds(h * GRP, GRP)].reshape(rows, HD), preferred_element_type=jnp.float32
        )
        spread = jnp.zeros((slots, HD), jnp.float32)
        for g in range(GRP):
            spread = jnp.where(group_col == g, lse_r[h * GRP + g], spread)
        far_top = jnp.sum(jnp.where(lane == rank_col, spread, 0.0), axis=1, keepdims=True)
        top = own_top[h]
        joint = jnp.maximum(far_top, top)
        far_weight = jnp.exp2(far_top - joint)
        own_weight = jnp.exp2(top - joint)
        below = far_weight + own_weight * own_sum[h]
        mixed[:, cols] = (far_weight * far + own_weight * mixed[:, cols]) / below

    @pl.loop(0, slots // 16)
    def _(r):
        some = pl.ds(pl.multiple_of(r * 16, 16), 16)
        summed = x_ref[some, :].astype(jnp.float32) + mixed[some, :]
        hid_ref[some, :] = norm_rows(summed, gain_ref[...], shift_ref[...]).astype(jnp.bfloat16)

    wait_bytes(qs.at[pl.ds(0, GRP * DEV - 1)], q_send)
    wait_bytes(ans_s.at[pl.ds(0, GRP * DEV - 1)], a_send)
    wait_bytes(lse_s.at[pl.ds(0, GRP * DEV - 1)], l_send)
    wait_bytes(bias_r.at[pl.ds(0, NC * DEV - 1)], b_send)


def mlp_kernel(
    hid_ref, bias_ref, up_ref, down_ref, dbias_ref, gain_ref, shift_ref,
    out_ref,
    tok, wu, wd, hidden, acc, part_s, part_r,
    w_sem, w_send, w_recv, t_send, t_recv, p_send, p_recv,
):
    y, c, x, z = coordinates()
    slots, width = hid_ref.shape
    steps_y = (0, 1, 3, 2)
    back = {1: 2, 2: 1, 3: 3}

    def at_y(pos):
        return place(lax.rem(y + steps_y[pos], NY), c, x, z)

    partner = place(y, 1 - c, x, z)
    barrier = pltpu.get_barrier_semaphore()
    for pos in (1, 2, 3):
        pl.semaphore_signal(barrier, inc=1, device_id=at_y(pos), device_id_type=MESH)
    pl.semaphore_signal(barrier, inc=1, device_id=partner, device_id_type=MESH)
    own_up = pltpu.make_async_copy(up_ref, wu.at[0], w_sem.at[0])
    own_down = pltpu.make_async_copy(down_ref, wd.at[0], w_sem.at[1])
    own_up.start()
    own_down.start()
    tok[0:slots, :] = hid_ref[...]
    pl.semaphore_wait(barrier, NY)

    def remote(src, dst, send_sem, recv_sem, where):
        return pltpu.make_async_remote_copy(
            src_ref=src, dst_ref=dst, send_sem=send_sem, recv_sem=recv_sem,
            device_id=where, device_id_type=MESH,
        )

    token_copies = {
        pos: remote(
            hid_ref, tok.at[pl.ds(back[pos] * slots, slots)],
            t_send.at[pos - 1], t_recv.at[back[pos] - 1], at_y(pos),
        )
        for pos in (1, 2, 3)
    }
    for pos in (3, 1, 2):
        token_copies[pos].start()
    weight_copies = (
        remote(up_ref, wu.at[1], w_send.at[0], w_recv.at[0], partner),
        remote(down_ref, wd.at[1], w_send.at[1], w_recv.at[1], partner),
    )
    for copy in weight_copies:
        copy.start()

    tile = 256
    units = wu.shape[2]

    def half_mlp(first, count, slot):
        rows = pl.ds(first * slots, count * slots)
        which = c if slot == 0 else 1 - c

        @pl.loop(0, units // tile)
        def _(n):
            cols = pl.ds(pl.multiple_of(n * tile, tile), tile)
            u = jnp.dot(tok[rows, :], wu[slot, :, cols], preferred_element_type=jnp.float32)
            u = u + bias_ref[pl.ds(which, 1), cols]
            hidden[rows, cols] = jax.nn.gelu(u, approximate=True).astype(jnp.bfloat16)

        @pl.loop(0, width // tile)
        def _(n):
            cols = pl.ds(pl.multiple_of(n * tile, tile), tile)
            m = jnp.dot(hidden[rows, :], wd[slot, :, cols], preferred_element_type=jnp.float32)
            if slot == 0:
                acc[rows, cols] = m
            else:
                acc[rows, cols] += m

    def send_partial(pos):
        part_s[pos - 1] = acc[pl.ds(pos * slots, slots), :].astype(jnp.bfloat16)
        copy = remote(
            part_s.at[pos - 1], part_r.at[back[pos] - 1], p_send.at[pos - 1], p_recv.at[back[pos] - 1], at_y(pos)
        )
        copy.start()
        return copy

    own_up.wait()
    own_down.wait()
    half_mlp(0, 1, 0)
    wait_bytes(tok.at[pl.ds(slots, slots)], t_recv.at[0])
    wait_bytes(tok.at[pl.ds(2 * slots, slots)], t_recv.at[1])
    half_mlp(1, 2, 0)
    wait_bytes(wu.at[1], w_recv.at[0])
    wait_bytes(wd.at[1], w_recv.at[1])
    half_mlp(1, 2, 1)
    partials = [send_partial(1), send_partial(2)]
    wait_bytes(tok.at[pl.ds(3 * slots, slots)], t_recv.at[2])
    half_mlp(3, 1, 0)
    half_mlp(3, 1, 1)
    partials.append(send_partial(3))
    half_mlp(0, 1, 1)
    for pos in (1, 2, 3):
        wait_bytes(part_r.at[pos - 1], p_recv.at[pos - 1])

    @pl.loop(0, slots // 16)
    def _(r):
        some = pl.ds(pl.multiple_of(r * 16, 16), 16)
        total = acc[some, :] + hid_ref[some, :].astype(jnp.float32) + dbias_ref[...]
        for pos in range(3):
            total = total + part_r[pos, some, :].astype(jnp.float32)
        out_ref[some, :] = norm_rows(total, gain_ref[...], shift_ref[...]).astype(jnp.bfloat16)

    for copy in partials:
        copy.wait_send()
    for pos in (1, 2, 3):
        token_copies[pos].wait_send()
    for copy in weight_copies:
        copy.wait_send()


def vmem():
    return pl.BlockSpec(memory_space=pltpu.VMEM)


def on_device(
    queries, keys, values, layer_input, lengths, groups, prefix_keys, prefix_values,
    up_weight, up_bias, down_weight, down_bias, attn_gain, attn_shift, out_gain, out_shift,
):
    slots, width = queries.shape
    heads = width // HD
    plen = prefix_keys.shape[1]
    rows = GRP * CAP
    local = up_bias.shape[0]
    odd = lax.rem(lax.axis_index("z"), 2)
    bias_line = up_bias.astype(jnp.float32)[None]
    blank = jnp.zeros_like(bias_line)
    bias_line = jnp.concatenate(
        [jnp.where(odd == 0, bias_line, blank), jnp.where(odd == 0, blank, bias_line)], axis=1
    )
    up_half = lax.all_gather(up_weight, ("x", "z"), axis=1, tiled=True)
    down_half = lax.all_gather(down_weight, ("x", "z"), axis=0, tiled=True)
    f32, bf16 = jnp.float32, jnp.bfloat16
    dma = pltpu.SemaphoreType.DMA
    smem = pl.BlockSpec(memory_space=pltpu.SMEM)
    hidden_state, bias_all = pl.pallas_call(
        prefix_kernel,
        out_shape=(
            jax.ShapeDtypeStruct((slots, width), bf16),
            jax.ShapeDtypeStruct((NC, DEV * local), f32),
        ),
        in_specs=[smem, smem] + [vmem()] * 9,
        out_specs=(vmem(), vmem()),
        scratch_shapes=[
            pltpu.VMEM((GRP * DEV, CAP, HD), bf16),
            pltpu.VMEM((GRP * DEV, CAP, HD), bf16),
            pltpu.VMEM((GRP * DEV, CAP, HD), bf16),
            pltpu.VMEM((GRP * DEV, CAP, HD), bf16),
            pltpu.VMEM((GRP * DEV, 1, HD), f32),
            pltpu.VMEM((GRP * DEV, 1, HD), f32),
            pltpu.VMEM((NC * DEV, 1, HD), f32),
            pltpu.VMEM((rows, plen), f32),
            pltpu.VMEM((rows, plen), f32),
            pltpu.VMEM((rows, plen), bf16),
            pltpu.VMEM((rows, plen), bf16),
            pltpu.VMEM((rows, HD), f32),
            pltpu.VMEM((2, rows, 1), f32),
            pltpu.VMEM((2, rows, 1), f32),
            pltpu.VMEM((slots, width), f32),
            pltpu.VMEM((heads, slots, 1), f32),
            pltpu.VMEM((heads, slots, 1), f32),
            dma, dma((DEV,)), dma, dma, dma, dma, dma, dma, dma((4,)),
        ],
        compiler_params=pltpu.CompilerParams(collective_id=0, has_side_effects=True, vmem_limit_bytes=LIMIT),
        cost_estimate=pl.CostEstimate(flops=20_000_000_000, bytes_accessed=8_000_000, transcendentals=17_000_000),
        name="prefix",
    )(
        lengths, groups, queries, keys, values, layer_input, bias_line,
        prefix_keys[0], prefix_values[0], attn_gain[None], attn_shift[None],
    )
    units = DEV * local
    anywhere = pl.BlockSpec(memory_space=pl.ANY)
    return pl.pallas_call(
        mlp_kernel,
        out_shape=jax.ShapeDtypeStruct((slots, width), bf16),
        in_specs=[vmem(), vmem(), anywhere, anywhere, vmem(), vmem(), vmem()],
        out_specs=vmem(),
        scratch_shapes=[
            pltpu.VMEM((NY * slots, width), bf16),
            pltpu.VMEM((NC, width, units), bf16),
            pltpu.VMEM((NC, units, width), bf16),
            pltpu.VMEM((NY * slots, units), bf16),
            pltpu.VMEM((NY * slots, width), f32),
            pltpu.VMEM((3, slots, width), bf16),
            pltpu.VMEM((3, slots, width), bf16),
            dma((2,)), dma((2,)), dma((2,)), dma((3,)), dma((3,)), dma((3,)), dma((3,)),
        ],
        compiler_params=pltpu.CompilerParams(collective_id=1, has_side_effects=True, vmem_limit_bytes=LIMIT),
        name="mlp",
    )(hidden_state, bias_all, up_half, down_half, down_bias[None], out_gain[None], out_shift[None])


def solution(mesh):
    fine = Mesh(mesh.devices.reshape(NY, NC, NX, NZ), ("y", "c", "x", "z"))
    grp, dev = ("y", "c"), ("x", "z")
    every = grp + dev
    token_rows = P(every, None)
    placed = (
        (token_rows,) * 6
        + (P(grp, None, dev),) * 2
        + (P(None, every), P(every), P(every, None))
        + (P(),) * 5
    )
    return jax.shard_map(on_device, mesh=fine, in_specs=placed, out_specs=token_rows, check_vma=False)
```

```python
import functools

import jax
import jax.numpy as jnp
from jax import lax
from jax.experimental import pallas as pl
from jax.experimental.pallas import tpu as pltpu
from jax.sharding import Mesh, PartitionSpec as P

HD = 128
NY, NC, NX, NZ = 4, 2, 4, 4
GRP, DEV = NY * NC, NX * NZ
CAP = 32
LOG2E = 1.4426950408889634
SCALE2 = HD**-0.5 * LOG2E
NORM_EPS = 1e-12
NEG = -1e30
MESH = pl.DeviceIdType.MESH
NT_DIMS = (((1,), (1,)), ((), ()))
LIMIT = 64 * 1024 * 1024 - 65536


def coordinates():
    return tuple(lax.axis_index(name) for name in ("y", "c", "x", "z"))


def place(y, c, x, z):
    return {"y": y, "c": c, "x": x, "z": z}


def plane_at(x, z, block):
    return lax.rem(x + block // NZ, NX), lax.rem(z + lax.rem(block, NZ), NZ)


def plane_back(x, z, block):
    return lax.rem(x + NX - block // NZ, NX), lax.rem(z + NZ - lax.rem(block, NZ), NZ)


def block_index(x, z, c):
    return z * (NC * NX) + c * NX + x


def wait_bytes(ref, sem):
    pltpu.make_async_copy(ref, ref, sem).wait()


def norm_rows(summed, gain, shift):
    mean = jnp.mean(summed, axis=-1, keepdims=True)
    centred = summed - mean
    spread = jnp.mean(centred * centred, axis=-1, keepdims=True)
    return centred * lax.rsqrt(spread + NORM_EPS) * gain + shift


def slot_tables(len_ref, grp_ref, shape, dim):
    slot = lax.broadcasted_iota(jnp.int32, shape, dim)
    start = jnp.int32(0)
    group = jnp.zeros(shape, jnp.int32)
    rank = jnp.zeros(shape, jnp.int32)
    for request in range(len_ref.shape[1]):
        length = len_ref[0, request]
        inside = (slot >= start) & (slot < start + length)
        group = jnp.where(inside, grp_ref[0, request], group)
        rank = jnp.where(inside, slot - start, rank)
        start = start + length
    return group, rank


def layer_kernel(
    len_ref, grp_ref, q_ref, bias_ref, k_in, v_in, x_in, pk_in, pv_in, up_in, down_in,
    again_ref, ashift_ref, dbias_ref, ogain_ref, oshift_ref,
    out_ref,
    k_ref, v_ref, x_ref, pk_ref, pv_ref,
    qs, qr, ans_s, ans_r, lse_s, lse_r, bias_s, bias_r, bias_all,
    s0, s1, p0, p1, acc, peak, tops, sums, mixed, own_top, own_sum,
    wu, wd, tok, hidden, total_acc, half_s, half_r, part_s, part_r,
    q_send, q_recv, a_send, a_recv, l_send, l_recv, b_send, b_recv, self_sem, in_sem,
    w_send, w_recv, w_cross, t_send, t_recv, h_send, h_recv, p_send, p_recv,
):
    y, c, x, z = coordinates()
    me_g = y * NC + c
    me_d = x * NZ + z
    slots = q_ref.shape[0]
    heads = q_ref.shape[1] // HD
    s_bufs, p_bufs = (s0, s1), (p0, p1)
    rows = GRP * CAP
    plen = pk_ref.shape[0]

    def group_at(k):
        g = lax.rem(me_g + k, GRP)
        return g, g // NC, lax.rem(g, NC)

    loads = [
        pltpu.make_async_copy(src, dst, in_sem.at[n])
        for n, (src, dst) in enumerate(
            ((k_in, k_ref), (v_in, v_ref), (pk_in, pk_ref), (pv_in, pv_ref), (x_in, x_ref))
        )
    ]
    for load in loads:
        load.start()
    barrier = pltpu.get_barrier_semaphore()

    def greet(block, k):
        tx, tz = plane_at(x, z, block)
        _, ty, tc = group_at(k)
        pl.semaphore_signal(barrier, inc=1, device_id=place(ty, tc, tx, tz), device_id_type=MESH)

    for k in range(1, GRP):
        greet(0, k)

    @pl.loop(1, DEV)
    def _(block):
        for k in range(GRP):
            greet(block, k)

    group_row, rank_row = slot_tables(len_ref, grp_ref, (1, slots), 1)
    pick = lax.broadcasted_iota(jnp.int32, (rows, slots), 0) == group_row * CAP + rank_row
    pick = pick.astype(jnp.float32).astype(jnp.bfloat16)
    line = bias_ref[...].astype(jnp.float32)
    line = jnp.concatenate([line, line], axis=1)
    side = lax.broadcasted_iota(jnp.int32, line.shape, 1) // (HD // 2)
    bias_s[...] = jnp.where(side == lax.rem(x, 2), line, 0.0)
    for d in range(heads):
        packed = jnp.dot(pick, q_ref[:, d * HD : (d + 1) * HD], preferred_element_type=jnp.float32)
        packed = packed.astype(jnp.bfloat16).reshape(GRP, CAP, HD)
        for g in range(GRP):
            qs[g * DEV + d] = packed[g]
    pl.semaphore_wait(barrier, GRP * DEV - 1)

    weights = (wu, wd)
    sources = (up_in, down_in)
    ring_steps = (0, -1, 1, 2)

    def block_of(ab, r1, r2, core):
        rx, rz = (r1, r2) if ab == 0 else (r2, r1)
        return block_index(lax.rem(x + rx + NX, NX), lax.rem(z + rz + NZ, NZ), core)

    def along(ab, axis, step):
        if (ab + axis) % 2 == 0:
            return place(y, c, lax.rem(x + step + NX, NX), z)
        return place(y, c, x, lax.rem(z + step + NZ, NZ))

    partner = place(y, 1 - c, x, z)

    def weight_part(ab, r1, r2, part):
        block = weights[ab].at[block_of(ab, r1, r2, c)]
        return block if part is None else block.at[pl.ds(part * 32, 32)]

    def weight_send(ab, r1, r2, part, axis, step, phase, kind):
        dst = weight_part(ab, r1, r2, part)
        src = sources[ab] if (r1 == 0 and r2 == 0) else dst
        pltpu.make_async_remote_copy(
            src_ref=src, dst_ref=dst, send_sem=w_send.at[ab], recv_sem=w_recv.at[ab, phase, kind],
            device_id=along(ab, axis, step), device_id_type=MESH,
        ).start()

    def weight_cross(ab, r1, r2):
        block = weight_part(ab, r1, r2, None)
        src = sources[ab] if (r1 == 0 and r2 == 0) else block
        pltpu.make_async_remote_copy(
            src_ref=src, dst_ref=block, send_sem=w_send.at[ab], recv_sem=w_cross.at[ab, ring_steps.index(r2)],
            device_id=partner, device_id_type=MESH,
        ).start()

    def weight_wait(ab, phase, kind):
        ref = weights[ab].at[0]
        wait_bytes(ref if kind < 2 else ref.at[pl.ds(0, 32)], w_recv.at[ab, phase, kind])

    def first_own(ab):
        weight_send(ab, 0, 0, None, 0, 1, 0, 0)
        weight_send(ab, 0, 0, None, 0, -1, 0, 1)

    def first_direct(ab):
        weight_wait(ab, 0, 0)
        weight_send(ab, -1, 0, 0, 0, 1, 0, 2)
        weight_wait(ab, 0, 1)
        weight_send(ab, 1, 0, 1, 0, -1, 0, 3)
        weight_cross(ab, -1, 0)
        weight_cross(ab, 1, 0)

    def first_half(ab):
        weight_wait(ab, 0, 2)
        weight_wait(ab, 0, 3)
        weight_cross(ab, 2, 0)

    def second_own(ab, k):
        weight_send(ab, ring_steps[k], 0, None, 1, 1, 1 + k, 0)
        weight_send(ab, ring_steps[k], 0, None, 1, -1, 1 + k, 1)

    def second_direct(ab, k):
        r1 = ring_steps[k]
        weight_wait(ab, 1 + k, 0)
        weight_send(ab, r1, -1, 0, 1, 1, 1 + k, 2)
        weight_wait(ab, 1 + k, 1)
        weight_send(ab, r1, 1, 1, 1, -1, 1 + k, 3)
        weight_cross(ab, r1, -1)
        weight_cross(ab, r1, 1)

    def second_half(ab, k):
        weight_wait(ab, 1 + k, 2)
        weight_wait(ab, 1 + k, 3)
        weight_cross(ab, ring_steps[k], 2)

    own_weights = [
        pltpu.make_async_copy(sources[ab], weights[ab].at[block_of(ab, 0, 0, c)], in_sem.at[5 + ab])
        for ab in range(2)
    ]

    def weights_begin():
        for ab in range(2):
            own_weights[ab].start()
            first_own(ab)
            weight_cross(ab, 0, 0)
        for ab in range(2):
            second_own(ab, 0)

    def weights_1():
        for ab in range(2):
            first_direct(ab)
        for ab in range(2):
            second_own(ab, 1)
            second_own(ab, 2)

    def weights_2():
        for ab in range(2):
            second_direct(ab, 0)
            first_half(ab)
            second_own(ab, 3)

    def weights_3():
        for ab in range(2):
            second_half(ab, 0)
            second_direct(ab, 1)
            second_direct(ab, 2)

    def weights_4():
        for ab in range(2):
            second_direct(ab, 3)

    def weights_5(ab):
        for k in (1, 2, 3):
            second_half(ab, k)

    def cross_wait(ab, r2):
        wait_bytes(weights[ab].at[pl.ds(0, 4)], w_cross.at[ab, ring_steps.index(r2)])

    def send_query(block, k):
        tx, tz = plane_at(x, z, block)
        g, ty, tc = group_at(k)
        pltpu.make_async_remote_copy(
            src_ref=qs.at[g * DEV + tx * NZ + tz],
            dst_ref=qr.at[block * GRP + me_g],
            send_sem=q_send,
            recv_sem=q_recv.at[block],
            device_id=place(ty, tc, tx, tz),
            device_id_type=MESH,
        ).start()

    own_query = pltpu.make_async_copy(qs.at[me_g * DEV + me_d], qr.at[me_g], self_sem.at[0])
    own_query.start()
    for k in range(1, GRP):
        send_query(0, k)

    @pl.loop(1, DEV)
    def _(block):
        for k in range(GRP):
            send_query(block, k)

    for k in range(1, NC * DEV):
        tc = lax.rem(c + k // DEV, NC)
        tx, tz = plane_at(x, z, k % DEV)
        pltpu.make_async_remote_copy(
            src_ref=bias_s,
            dst_ref=bias_r.at[block_index(x, z, c)],
            send_sem=b_send,
            recv_sem=b_recv,
            device_id=place(y, tc, tx, tz),
            device_id_type=MESH,
        ).start()
    own_bias = pltpu.make_async_copy(bias_s, bias_r.at[block_index(x, z, c)], self_sem.at[3])
    own_bias.start()
    weights_begin()
    loads[0].wait()
    loads[1].wait()

    group_col, rank_col = slot_tables(len_ref, grp_ref, (slots, 1), 0)
    visible = (group_col == group_row) & (
        lax.broadcasted_iota(jnp.int32, (slots, slots), 1)
        <= lax.broadcasted_iota(jnp.int32, (slots, slots), 0)
    )

    @pl.loop(0, heads)
    def _(h):
        cols = pl.ds(pl.multiple_of(h * HD, HD), HD)
        s = lax.dot_general(q_ref[:, cols], k_ref[:, cols], NT_DIMS, preferred_element_type=jnp.float32)
        s = jnp.where(visible, s * SCALE2, NEG)
        top = jnp.max(s, axis=1, keepdims=True)
        w = jnp.where(visible, jnp.exp2(s - top), 0.0)
        own_top[h] = top
        own_sum[h] = jnp.sum(w, axis=1, keepdims=True)
        mixed[:, cols] = jnp.dot(w.astype(jnp.bfloat16), v_ref[:, cols], preferred_element_type=jnp.float32)

    def answer_back(block, k):
        tx, tz = plane_back(x, z, block)
        g, ty, tc = group_at(k)
        where = place(ty, tc, tx, tz)
        pltpu.make_async_remote_copy(
            src_ref=ans_s.at[block * GRP + g],
            dst_ref=ans_r.at[me_d * GRP + me_g],
            send_sem=a_send, recv_sem=a_recv, device_id=where, device_id_type=MESH,
        ).start()
        pltpu.make_async_remote_copy(
            src_ref=lse_s.at[block * GRP + g],
            dst_ref=lse_r.at[me_d * GRP + me_g],
            send_sem=l_send, recv_sem=l_recv, device_id=where, device_id_type=MESH,
        ).start()

    steps = 4
    span = plen // steps
    part = rows // steps

    def stage(i, parity, scoring, weighing, mixing, first=False):
        other = 1 - parity
        if scoring:
            if first:
                wait_bytes(qr.at[pl.ds(0, GRP - 1)], q_recv.at[0])
                own_query.wait()
            else:
                wait_bytes(qr.at[pl.ds(i * GRP, GRP)], q_recv.at[i])
            peak[...] = jnp.full_like(peak, NEG)
        if mixing:
            acc[...] = jnp.zeros_like(acc)

        @pl.loop(0, steps)
        def _(j):
            keys = pl.ds(pl.multiple_of(j * span, span), span)
            if scoring:
                block = qr[pl.ds(i * GRP, GRP)].reshape(rows, HD)
                s = lax.dot_general(block, pk_ref[keys, :], NT_DIMS, preferred_element_type=jnp.float32)
                s_bufs[parity][:, keys] = s
                high = s[:, :HD]
                for t in range(1, span // HD):
                    high = jnp.maximum(high, s[:, t * HD : (t + 1) * HD])
                peak[...] = jnp.maximum(peak[...], high)
            if weighing:
                some = pl.ds(pl.multiple_of(j * part, part), part)
                top = tops[other, some, :]
                total = jnp.zeros((part, HD), jnp.float32)
                for t in range(plen // HD):
                    cols = slice(t * HD, (t + 1) * HD)
                    w = jnp.exp2(s_bufs[other][some, cols] * SCALE2 - top)
                    total = total + w
                    p_bufs[other][some, cols] = w.astype(jnp.bfloat16)
                sums[other, some, :] = total
            if mixing:
                acc[...] += jnp.dot(p_bufs[parity][:, keys], pv_ref[keys, :], preferred_element_type=jnp.float32)

        if mixing:
            done = i - 2
            total = jnp.sum(sums[parity], axis=1, keepdims=True)
            answer = (acc[...] / total).astype(jnp.bfloat16).reshape(GRP, CAP, HD)
            spread = (tops[parity] + jnp.log(total) * LOG2E).reshape(GRP, CAP, HD)
            diagonal = lax.broadcasted_iota(jnp.int32, (GRP, CAP, HD), 1) == lax.broadcasted_iota(
                jnp.int32, (GRP, CAP, HD), 2
            )
            lines = jnp.sum(jnp.where(diagonal, spread, 0.0), axis=1)
            for g in range(GRP):
                ans_s[done * GRP + g] = answer[g]
                lse_s[done * GRP + g] = lines[g : g + 1]
        if scoring:
            tops[parity] = jnp.broadcast_to(jnp.max(peak[...], axis=1, keepdims=True) * SCALE2, (rows, HD))

    def send_back(done):
        for k in range(GRP):
            answer_back(done, k)

    loads[2].wait()
    loads[3].wait()
    stage(0, 0, True, False, False, first=True)
    stage(1, 1, True, True, False)
    stage(2, 0, True, True, True)
    own_answer = pltpu.make_async_copy(ans_s.at[me_g], ans_r.at[me_d * GRP + me_g], self_sem.at[1])
    own_lse = pltpu.make_async_copy(lse_s.at[me_g], lse_r.at[me_d * GRP + me_g], self_sem.at[2])
    own_answer.start()
    own_lse.start()
    for k in range(1, GRP):
        answer_back(0, k)
    stage(3, 1, True, True, True)
    send_back(1)

    def stage_pairs(first_pair, last_pair):
        @pl.loop(first_pair, last_pair)
        def _(pair):
            stage(2 * pair, 0, True, True, True)
            send_back(2 * pair - 2)
            stage(2 * pair + 1, 1, True, True, True)
            send_back(2 * pair - 1)

    stage_pairs(2, 4)
    weights_1()
    stage_pairs(4, 6)
    weights_2()
    stage_pairs(6, 8)
    weights_3()
    stage(DEV, 0, False, True, True)
    send_back(DEV - 2)
    stage(DEV + 1, 1, False, False, True)
    send_back(DEV - 1)

    own_bias.wait()
    wait_bytes(bias_r.at[pl.ds(0, NC * DEV - 1)], b_recv)
    for e in range(NC * DEV // 2):
        bias_all[:, e * HD : (e + 1) * HD] = bias_r[2 * e] + bias_r[2 * e + 1]

    weights_4()
    own_answer.wait()
    own_lse.wait()
    wait_bytes(ans_r.at[pl.ds(0, GRP * DEV - 1)], a_recv)
    wait_bytes(lse_r.at[pl.ds(0, GRP * DEV - 1)], l_recv)
    unpick = lax.broadcasted_iota(jnp.int32, (slots, rows), 1) == group_col * CAP + rank_col
    unpick = unpick.astype(jnp.float32).astype(jnp.bfloat16)
    lane = lax.broadcasted_iota(jnp.int32, (slots, HD), 1)

    @pl.loop(0, heads)
    def _(h):
        cols = pl.ds(pl.multiple_of(h * HD, HD), HD)
        far = jnp.dot(
            unpick, ans_r[pl.ds(h * GRP, GRP)].reshape(rows, HD), preferred_element_type=jnp.float32
        )
        spread = jnp.zeros((slots, HD), jnp.float32)
        for g in range(GRP):
            spread = jnp.where(group_col == g, lse_r[h * GRP + g], spread)
        far_top = jnp.sum(jnp.where(lane == rank_col, spread, 0.0), axis=1, keepdims=True)
        top = own_top[h]
        joint = jnp.maximum(far_top, top)
        far_weight = jnp.exp2(far_top - joint)
        own_weight = jnp.exp2(top - joint)
        below = far_weight + own_weight * own_sum[h]
        mixed[:, cols] = (far_weight * far + own_weight * mixed[:, cols]) / below

    loads[4].wait()

    @pl.loop(0, slots // 16)
    def _(r):
        some = pl.ds(pl.multiple_of(r * 16, 16), 16)
        summed = x_ref[some, :].astype(jnp.float32) + mixed[some, :]
        tok[some, :] = norm_rows(summed, again_ref[...], ashift_ref[...]).astype(jnp.bfloat16)

    def y_copy(src, dst, send_sem, recv_sem, step):
        return pltpu.make_async_remote_copy(
            src_ref=src, dst_ref=dst, send_sem=send_sem, recv_sem=recv_sem,
            device_id=place(lax.rem(y + step + NY, NY), c, x, z), device_id_type=MESH,
        )

    def token(pos, part=None):
        return tok.at[pl.ds(pos * slots, slots)] if part is None else tok.at[
            pl.ds(pos * slots + part * (slots // 2), slots // 2)
        ]

    sent = [
        y_copy(token(0), token(2), t_send.at[0], t_recv.at[0], 1),
        y_copy(token(0), token(1), t_send.at[1], t_recv.at[1], -1),
    ]
    sent[0].start()
    sent[1].start()
    own_weights[0].wait()
    own_weights[1].wait()
    width = q_ref.shape[1]
    tile = 256
    per_tile = tile // 64

    def up(first, count, r2):
        rows_ = pl.ds(first * slots, count * slots)
        base = lax.rem(z + r2 + NZ, NZ) * (NC * NX)

        @pl.loop(0, NC * NX // per_tile)
        def _(n):
            block = base + n * per_tile
            cols = pl.ds(pl.multiple_of(block * 64, tile), tile)
            u = lax.dot_general(
                tok[rows_, :], wu[pl.ds(block, per_tile)].reshape(tile, width), NT_DIMS,
                preferred_element_type=jnp.float32,
            )
            u = u + bias_all[:, cols]
            hidden[rows_, cols] = jax.nn.gelu(u, approximate=True).astype(jnp.bfloat16)

    def down(first, count):
        rows_ = pl.ds(first * slots, count * slots)

        @pl.loop(0, width // tile)
        def _(n):
            cols = pl.ds(pl.multiple_of(n * tile, tile), tile)
            total_acc[rows_, cols] = jnp.dot(
                hidden[rows_, :], wd[:, :, cols].reshape(NC * DEV * 64, tile),
                preferred_element_type=jnp.float32,
            )

    cross_wait(0, 0)
    up(0, 1, 0)
    wait_bytes(token(2), t_recv.at[0])
    wait_bytes(token(1), t_recv.at[1])
    sent.append(y_copy(token(2, 0), token(3, 0), t_send.at[2], t_recv.at[2], 1))
    sent.append(y_copy(token(1, 1), token(3, 1), t_send.at[3], t_recv.at[3], -1))
    sent[2].start()
    sent[3].start()
    weights_5(0)
    weights_5(1)
    for r2 in ring_steps[1:]:
        cross_wait(0, r2)
        up(0, 1, r2)
    for r2 in ring_steps:
        up(1, 2, r2)
    wait_bytes(token(3, 0), t_recv.at[2])
    wait_bytes(token(3, 1), t_recv.at[3])
    for r2 in ring_steps:
        up(3, 1, r2)
    for r2 in ring_steps:
        cross_wait(1, r2)
    down(3, 1)
    cut = width // 2
    for side in range(2):
        half_s[side] = total_acc[3 * slots :, side * cut : (side + 1) * cut].astype(jnp.bfloat16)
        sent.append(y_copy(half_s.at[side], half_r.at[side], h_send.at[side], h_recv.at[side], 1 - 2 * side))
        sent[-1].start()
    down(1, 2)
    for side in range(2):
        wait_bytes(half_r.at[side], h_recv.at[side])
        at = slice((1 + side) * slots, (2 + side) * slots)
        for half in range(2):
            cols = slice(half * cut, (half + 1) * cut)
            partial = total_acc[at, cols]
            if half == side:
                partial = partial + half_r[side].astype(jnp.float32)
            part_s[side, :, cols] = partial.astype(jnp.bfloat16)
        sent.append(y_copy(part_s.at[side], part_r.at[side], p_send.at[side], p_recv.at[side], 1 - 2 * side))
        sent[-1].start()
    down(0, 1)
    for side in range(2):
        wait_bytes(part_r.at[side], p_recv.at[side])

    @pl.loop(0, slots // 16)
    def _(r):
        some = pl.ds(pl.multiple_of(r * 16, 16), 16)
        total = total_acc[some, :] + tok[some, :].astype(jnp.float32) + dbias_ref[...]
        for side in range(2):
            total = total + part_r[side, some, :].astype(jnp.float32)
        out_ref[some, :] = norm_rows(total, ogain_ref[...], oshift_ref[...]).astype(jnp.bfloat16)

    for copy in sent:
        copy.wait_send()
    wait_bytes(qs.at[pl.ds(0, GRP * DEV - 1)], q_send)
    wait_bytes(ans_s.at[pl.ds(0, GRP * DEV - 1)], a_send)
    wait_bytes(lse_s.at[pl.ds(0, GRP * DEV - 1)], l_send)
    wait_bytes(bias_r.at[pl.ds(0, NC * DEV - 1)], b_send)
    for ab in range(2):
        wait_bytes(weights[ab].at[pl.ds(0, NC * DEV - 1)], w_send.at[ab])


def vmem():
    return pl.BlockSpec(memory_space=pltpu.VMEM)


def on_device(
    queries, keys, values, layer_input, lengths, groups, prefix_keys, prefix_values,
    up_weight, up_bias, down_weight, down_bias, attn_gain, attn_shift, out_gain, out_shift,
):
    slots, width = queries.shape
    heads = width // HD
    plen = prefix_keys.shape[1]
    rows = GRP * CAP
    local = up_bias.shape[0]
    units = NC * DEV * local
    f32, bf16 = jnp.float32, jnp.bfloat16
    dma = pltpu.SemaphoreType.DMA
    smem = pl.BlockSpec(memory_space=pltpu.SMEM)
    anywhere = pl.BlockSpec(memory_space=pl.ANY)
    messages = pltpu.VMEM((GRP * DEV, CAP, HD), bf16)
    lines = pltpu.VMEM((GRP * DEV, 1, HD), f32)
    return pl.pallas_call(
        layer_kernel,
        out_shape=jax.ShapeDtypeStruct((slots, width), bf16),
        in_specs=[smem] * 2 + [vmem()] * 2 + [anywhere] * 7 + [vmem()] * 5,
        out_specs=vmem(),
        scratch_shapes=[
            pltpu.VMEM((slots, width), bf16),
            pltpu.VMEM((slots, width), bf16),
            pltpu.VMEM((slots, width), bf16),
            pltpu.VMEM((plen, HD), bf16),
            pltpu.VMEM((plen, HD), bf16),
            messages, messages, messages, messages, lines, lines,
            pltpu.VMEM((1, HD), f32),
            pltpu.VMEM((NC * DEV, 1, HD), f32),
            pltpu.VMEM((1, units), f32),
            pltpu.VMEM((rows, plen), f32),
            pltpu.VMEM((rows, plen), f32),
            pltpu.VMEM((rows, plen), bf16),
            pltpu.VMEM((rows, plen), bf16),
            pltpu.VMEM((rows, HD), f32),
            pltpu.VMEM((rows, HD), f32),
            pltpu.VMEM((2, rows, HD), f32),
            pltpu.VMEM((2, rows, HD), f32),
            pltpu.VMEM((slots, width), f32),
            pltpu.VMEM((heads, slots, 1), f32),
            pltpu.VMEM((heads, slots, 1), f32),
            pltpu.VMEM((NC * DEV, local, width), bf16),
            pltpu.VMEM((NC * DEV, local, width), bf16),
            pltpu.VMEM((NY * slots, width), bf16),
            pltpu.VMEM((NY * slots, units), bf16),
            pltpu.VMEM((NY * slots, width), f32),
            pltpu.VMEM((2, slots, width // 2), bf16),
            pltpu.VMEM((2, slots, width // 2), bf16),
            pltpu.VMEM((2, slots, width), bf16),
            pltpu.VMEM((2, slots, width), bf16),
            dma, dma((DEV,)), dma, dma, dma, dma, dma, dma, dma((4,)), dma((7,)),
            dma((2,)), dma((2, 5, 4)), dma((2, 4)), dma((4,)), dma((4,)), dma((2,)), dma((2,)), dma((2,)), dma((2,)),
        ],
        compiler_params=pltpu.CompilerParams(collective_id=0, has_side_effects=True, vmem_limit_bytes=LIMIT),
        name="layer",
    )(
        lengths, groups, queries, up_bias[None], keys, values, layer_input,
        prefix_keys[0], prefix_values[0], up_weight.T, down_weight,
        attn_gain[None], attn_shift[None], down_bias[None], out_gain[None], out_shift[None],
    )


def solution(mesh):
    fine = Mesh(mesh.devices.reshape(NY, NC, NX, NZ), ("y", "c", "x", "z"))
    grp, dev = ("y", "c"), ("x", "z")
    every = grp + dev
    token_rows = P(every, None)
    placed = (
        (token_rows,) * 6
        + (P(grp, None, dev),) * 2
        + (P(None, every), P(every), P(every, None))
        + (P(),) * 5
    )
    return jax.shard_map(on_device, mesh=fine, in_specs=placed, out_specs=token_rows, check_vma=False)
```

```python
import functools

import jax
import jax.numpy as jnp
from jax import lax
from jax.experimental import pallas as pl
from jax.experimental.pallas import tpu as pltpu
from jax.sharding import Mesh, PartitionSpec as P

HD = 128
NY, NC, NX, NZ = 4, 2, 4, 4
GRP, DEV = NY * NC, NX * NZ
CAP = 32
LOG2E = 1.4426950408889634
SCALE2 = HD**-0.5 * LOG2E
NORM_EPS = 1e-12
NEG = -1e30
MESH = pl.DeviceIdType.MESH
NT_DIMS = (((1,), (1,)), ((), ()))
LIMIT = 64 * 1024 * 1024 - 65536


def coordinates():
    return tuple(lax.axis_index(name) for name in ("y", "c", "x", "z"))


def place(y, c, x, z):
    return {"y": y, "c": c, "x": x, "z": z}


def plane_at(x, z, block):
    return lax.rem(x + block // NZ, NX), lax.rem(z + lax.rem(block, NZ), NZ)


def plane_back(x, z, block):
    return lax.rem(x + NX - block // NZ, NX), lax.rem(z + NZ - lax.rem(block, NZ), NZ)


def block_index(x, z, c):
    return z * (NC * NX) + c * NX + x


def wait_bytes(ref, sem):
    pltpu.make_async_copy(ref, ref, sem).wait()


def norm_rows(summed, gain, shift):
    mean = jnp.mean(summed, axis=-1, keepdims=True)
    centred = summed - mean
    spread = jnp.mean(centred * centred, axis=-1, keepdims=True)
    return centred * lax.rsqrt(spread + NORM_EPS) * gain + shift


def slot_tables(len_ref, grp_ref, shape, dim):
    slot = lax.broadcasted_iota(jnp.int32, shape, dim)
    start = jnp.int32(0)
    group = jnp.zeros(shape, jnp.int32)
    rank = jnp.zeros(shape, jnp.int32)
    for request in range(len_ref.shape[1]):
        length = len_ref[0, request]
        inside = (slot >= start) & (slot < start + length)
        group = jnp.where(inside, grp_ref[0, request], group)
        rank = jnp.where(inside, slot - start, rank)
        start = start + length
    return group, rank


def layer_kernel(
    len_ref, grp_ref, q_ref, bias_ref, k_in, v_in, x_in, pk_in, pv_in, up_in, down_in,
    again_ref, ashift_ref, dbias_ref, ogain_ref, oshift_ref,
    out_ref,
    k_ref, v_ref, x_ref, pk_ref, pv_ref,
    qs, qr, ans_s, ans_r, lse_s, lse_r, bias_s, bias_r, bias_all,
    s0, s1, p0, p1, acc, peak, tops, sums, mixed, own_top, own_sum,
    wu, wd, tok, hidden, total_acc, half_s, half_r, part_s, part_r,
    q_send, q_recv, a_send, a_recv, l_send, l_recv, b_send, b_recv, self_sem, in_sem,
    w_send, w_recv, w_cross, t_send, t_recv, h_send, h_recv, p_send, p_recv,
):
    y, c, x, z = coordinates()
    me_g = y * NC + c
    me_d = x * NZ + z
    slots = q_ref.shape[0]
    heads = q_ref.shape[1] // HD
    s_bufs, p_bufs = (s0, s1), (p0, p1)
    rows = GRP * CAP
    plen = pk_ref.shape[0]

    def group_at(k):
        g = lax.rem(me_g + k, GRP)
        return g, g // NC, lax.rem(g, NC)

    loads = [
        pltpu.make_async_copy(src, dst, in_sem.at[n])
        for n, (src, dst) in enumerate(
            ((k_in, k_ref), (v_in, v_ref), (pk_in, pk_ref), (pv_in, pv_ref), (x_in, x_ref))
        )
    ]
    for load in loads:
        load.start()
    barrier = pltpu.get_barrier_semaphore()

    def greet(block, k):
        tx, tz = plane_at(x, z, block)
        _, ty, tc = group_at(k)
        pl.semaphore_signal(barrier, inc=1, device_id=place(ty, tc, tx, tz), device_id_type=MESH)

    for k in range(1, GRP):
        greet(0, k)

    @pl.loop(1, DEV)
    def _(block):
        for k in range(GRP):
            greet(block, k)

    group_row, rank_row = slot_tables(len_ref, grp_ref, (1, slots), 1)
    pick = lax.broadcasted_iota(jnp.int32, (rows, slots), 0) == group_row * CAP + rank_row
    pick = pick.astype(jnp.float32).astype(jnp.bfloat16)
    line = bias_ref[...].astype(jnp.float32)
    line = jnp.concatenate([line, line], axis=1)
    side = lax.broadcasted_iota(jnp.int32, line.shape, 1) // (HD // 2)
    bias_s[...] = jnp.where(side == lax.rem(x, 2), line, 0.0)
    for d in range(heads):
        packed = jnp.dot(pick, q_ref[:, d * HD : (d + 1) * HD], preferred_element_type=jnp.float32)
        packed = packed.astype(jnp.bfloat16).reshape(GRP, CAP, HD)
        for g in range(GRP):
            qs[g * DEV + d] = packed[g]
    pl.semaphore_wait(barrier, GRP * DEV - 1)

    weights = (wu, wd)
    sources = (up_in, down_in)
    ring_steps = (0, -1, 1, 2)
    strip = up_in.shape[0] // 2

    def block_of(q, r1, r2):
        rx, rz = (r1, r2) if q % 2 == 0 else (r2, r1)
        return block_index(lax.rem(x + rx + NX, NX), lax.rem(z + rz + NZ, NZ), c)

    def along(q, axis, step):
        if (q + axis) % 2 == 0:
            return place(y, c, lax.rem(x + step + NX, NX), z)
        return place(y, c, x, lax.rem(z + step + NZ, NZ))

    partner = place(y, 1 - c, x, z)

    def strip_of(block, q, part):
        first = (q % 2) * strip
        if part is None:
            return block.at[pl.ds(first, strip)]
        return block.at[pl.ds(first + part * (strip // 2), strip // 2)]

    def weight_refs(q, r1, r2, part):
        dst = strip_of(weights[q // 2].at[block_of(q, r1, r2)], q, part)
        src = strip_of(sources[q // 2], q, part) if (r1 == 0 and r2 == 0) else dst
        return src, dst

    def weight_send(q, r1, r2, part, axis, step, phase, kind):
        src, dst = weight_refs(q, r1, r2, part)
        pltpu.make_async_remote_copy(
            src_ref=src, dst_ref=dst, send_sem=w_send.at[q // 2], recv_sem=w_recv.at[q, phase, kind],
            device_id=along(q, axis, step), device_id_type=MESH,
        ).start()

    def weight_cross(q, r1, r2):
        src, dst = weight_refs(q, r1, r2, None)
        pltpu.make_async_remote_copy(
            src_ref=src, dst_ref=dst, send_sem=w_send.at[q // 2], recv_sem=w_cross.at[q // 2],
            device_id=partner, device_id_type=MESH,
        ).start()

    def weight_wait(q, phase, kind):
        size = strip if kind < 2 else strip // 2
        wait_bytes(weights[q // 2].at[0, pl.ds(0, size)], w_recv.at[q, phase, kind])

    def both(tensor):
        return (2 * tensor, 2 * tensor + 1)

    def first_own(tensor):
        for q in both(tensor):
            weight_send(q, 0, 0, None, 0, 1, 0, 0)
            weight_send(q, 0, 0, None, 0, -1, 0, 1)
            weight_cross(q, 0, 0)

    def first_direct(tensor):
        for q in both(tensor):
            weight_wait(q, 0, 0)
            weight_send(q, -1, 0, 0, 0, 1, 0, 2)
            weight_wait(q, 0, 1)
            weight_send(q, 1, 0, 1, 0, -1, 0, 3)
            weight_cross(q, -1, 0)
            weight_cross(q, 1, 0)

    def first_half(tensor):
        for q in both(tensor):
            weight_wait(q, 0, 2)
            weight_wait(q, 0, 3)
            weight_cross(q, 2, 0)

    def second_own(tensor, k):
        for q in both(tensor):
            weight_send(q, ring_steps[k], 0, None, 1, 1, 1 + k, 0)
            weight_send(q, ring_steps[k], 0, None, 1, -1, 1 + k, 1)

    def second_direct(tensor, k):
        r1 = ring_steps[k]
        for q in both(tensor):
            weight_wait(q, 1 + k, 0)
            weight_send(q, r1, -1, 0, 1, 1, 1 + k, 2)
            weight_wait(q, 1 + k, 1)
            weight_send(q, r1, 1, 1, 1, -1, 1 + k, 3)
            weight_cross(q, r1, -1)
            weight_cross(q, r1, 1)

    def second_half(tensor, k):
        for q in both(tensor):
            weight_wait(q, 1 + k, 2)
            weight_wait(q, 1 + k, 3)
            weight_cross(q, ring_steps[k], 2)

    def cross_wait(tensor):
        wait_bytes(weights[tensor].at[pl.ds(0, DEV)], w_cross.at[tensor])

    own_weights = [
        pltpu.make_async_copy(sources[ab], weights[ab].at[block_index(x, z, c)], in_sem.at[5 + ab])
        for ab in range(2)
    ]

    def send_query(block, k):
        tx, tz = plane_at(x, z, block)
        g, ty, tc = group_at(k)
        pltpu.make_async_remote_copy(
            src_ref=qs.at[g * DEV + tx * NZ + tz],
            dst_ref=qr.at[block * GRP + me_g],
            send_sem=q_send,
            recv_sem=q_recv.at[block],
            device_id=place(ty, tc, tx, tz),
            device_id_type=MESH,
        ).start()

    own_query = pltpu.make_async_copy(qs.at[me_g * DEV + me_d], qr.at[me_g], self_sem.at[0])
    own_query.start()
    for k in range(1, GRP):
        send_query(0, k)

    @pl.loop(1, DEV)
    def _(block):
        for k in range(GRP):
            send_query(block, k)

    for k in range(1, NC * DEV):
        tc = lax.rem(c + k // DEV, NC)
        tx, tz = plane_at(x, z, k % DEV)
        pltpu.make_async_remote_copy(
            src_ref=bias_s,
            dst_ref=bias_r.at[block_index(x, z, c)],
            send_sem=b_send,
            recv_sem=b_recv,
            device_id=place(y, tc, tx, tz),
            device_id_type=MESH,
        ).start()
    own_bias = pltpu.make_async_copy(bias_s, bias_r.at[block_index(x, z, c)], self_sem.at[3])
    own_bias.start()
    own_weights[0].start()
    own_weights[1].start()
    first_own(0)
    second_own(0, 0)
    loads[0].wait()
    loads[1].wait()

    group_col, rank_col = slot_tables(len_ref, grp_ref, (slots, 1), 0)
    visible = (group_col == group_row) & (
        lax.broadcasted_iota(jnp.int32, (slots, slots), 1)
        <= lax.broadcasted_iota(jnp.int32, (slots, slots), 0)
    )

    @pl.loop(0, heads)
    def _(h):
        cols = pl.ds(pl.multiple_of(h * HD, HD), HD)
        s = lax.dot_general(q_ref[:, cols], k_ref[:, cols], NT_DIMS, preferred_element_type=jnp.float32)
        s = jnp.where(visible, s * SCALE2, NEG)
        top = jnp.max(s, axis=1, keepdims=True)
        w = jnp.where(visible, jnp.exp2(s - top), 0.0)
        own_top[h] = top
        own_sum[h] = jnp.sum(w, axis=1, keepdims=True)
        mixed[:, cols] = jnp.dot(w.astype(jnp.bfloat16), v_ref[:, cols], preferred_element_type=jnp.float32)

    def answer_back(block, k):
        tx, tz = plane_back(x, z, block)
        g, ty, tc = group_at(k)
        where = place(ty, tc, tx, tz)
        pltpu.make_async_remote_copy(
            src_ref=ans_s.at[block * GRP + g],
            dst_ref=ans_r.at[me_d * GRP + me_g],
            send_sem=a_send, recv_sem=a_recv, device_id=where, device_id_type=MESH,
        ).start()
        pltpu.make_async_remote_copy(
            src_ref=lse_s.at[block * GRP + g],
            dst_ref=lse_r.at[me_d * GRP + me_g],
            send_sem=l_send, recv_sem=l_recv, device_id=where, device_id_type=MESH,
        ).start()

    steps = 4
    span = plen // steps
    part = rows // steps

    def stage(i, parity, scoring, weighing, mixing, first=False):
        other = 1 - parity
        if scoring:
            if first:
                wait_bytes(qr.at[pl.ds(0, GRP - 1)], q_recv.at[0])
                own_query.wait()
            else:
                wait_bytes(qr.at[pl.ds(i * GRP, GRP)], q_recv.at[i])
            peak[...] = jnp.full_like(peak, NEG)
        if mixing:
            acc[...] = jnp.zeros_like(acc)

        @pl.loop(0, steps)
        def _(j):
            keys = pl.ds(pl.multiple_of(j * span, span), span)
            if scoring:
                block = qr[pl.ds(i * GRP, GRP)].reshape(rows, HD)
                s = lax.dot_general(block, pk_ref[keys, :], NT_DIMS, preferred_element_type=jnp.float32)
                s_bufs[parity][:, keys] = s
                high = s[:, :HD]
                for t in range(1, span // HD):
                    high = jnp.maximum(high, s[:, t * HD : (t + 1) * HD])
                peak[...] = jnp.maximum(peak[...], high)
            if weighing:
                some = pl.ds(pl.multiple_of(j * part, part), part)
                top = tops[other, some, :]
                total = jnp.zeros((part, HD), jnp.float32)
                for t in range(plen // HD):
                    cols = slice(t * HD, (t + 1) * HD)
                    w = jnp.exp2(s_bufs[other][some, cols] * SCALE2 - top)
                    total = total + w
                    p_bufs[other][some, cols] = w.astype(jnp.bfloat16)
                sums[other, some, :] = total
            if mixing:
                acc[...] += jnp.dot(p_bufs[parity][:, keys], pv_ref[keys, :], preferred_element_type=jnp.float32)

        if mixing:
            done = i - 2
            total = jnp.sum(sums[parity], axis=1, keepdims=True)
            answer = (acc[...] / total).astype(jnp.bfloat16).reshape(GRP, CAP, HD)
            spread = (tops[parity] + jnp.log(total) * LOG2E).reshape(GRP, CAP, HD)
            diagonal = lax.broadcasted_iota(jnp.int32, (GRP, CAP, HD), 1) == lax.broadcasted_iota(
                jnp.int32, (GRP, CAP, HD), 2
            )
            lines = jnp.sum(jnp.where(diagonal, spread, 0.0), axis=1)
            for g in range(GRP):
                ans_s[done * GRP + g] = answer[g]
                lse_s[done * GRP + g] = lines[g : g + 1]
        if scoring:
            tops[parity] = jnp.broadcast_to(jnp.max(peak[...], axis=1, keepdims=True) * SCALE2, (rows, HD))

    def send_back(done):
        for k in range(GRP):
            answer_back(done, k)

    loads[2].wait()
    loads[3].wait()
    stage(0, 0, True, False, False, first=True)
    stage(1, 1, True, True, False)
    stage(2, 0, True, True, True)
    own_answer = pltpu.make_async_copy(ans_s.at[me_g], ans_r.at[me_d * GRP + me_g], self_sem.at[1])
    own_lse = pltpu.make_async_copy(lse_s.at[me_g], lse_r.at[me_d * GRP + me_g], self_sem.at[2])
    own_answer.start()
    own_lse.start()
    for k in range(1, GRP):
        answer_back(0, k)
    stage(3, 1, True, True, True)
    send_back(1)

    def stage_pairs(first_pair, last_pair):
        @pl.loop(first_pair, last_pair)
        def _(pair):
            stage(2 * pair, 0, True, True, True)
            send_back(2 * pair - 2)
            stage(2 * pair + 1, 1, True, True, True)
            send_back(2 * pair - 1)

    stage_pairs(2, 4)
    first_direct(0)
    second_own(0, 1)
    second_own(0, 2)
    stage_pairs(4, 6)
    second_direct(0, 0)
    first_half(0)
    second_own(0, 3)
    stage_pairs(6, 8)
    second_direct(0, 1)
    second_direct(0, 2)
    stage(DEV, 0, False, True, True)
    send_back(DEV - 2)
    stage(DEV + 1, 1, False, False, True)
    send_back(DEV - 1)

    own_bias.wait()
    wait_bytes(bias_r.at[pl.ds(0, NC * DEV - 1)], b_recv)
    for e in range(NC * DEV // 2):
        bias_all[:, e * HD : (e + 1) * HD] = bias_r[2 * e] + bias_r[2 * e + 1]

    first_own(1)
    second_own(1, 0)
    second_half(0, 0)
    second_direct(0, 3)
    first_direct(1)
    second_own(1, 1)
    second_own(1, 2)
    own_answer.wait()
    own_lse.wait()
    wait_bytes(ans_r.at[pl.ds(0, GRP * DEV - 1)], a_recv)
    wait_bytes(lse_r.at[pl.ds(0, GRP * DEV - 1)], l_recv)
    unpick = lax.broadcasted_iota(jnp.int32, (slots, rows), 1) == group_col * CAP + rank_col
    unpick = unpick.astype(jnp.float32).astype(jnp.bfloat16)
    lane = lax.broadcasted_iota(jnp.int32, (slots, HD), 1)

    @pl.loop(0, heads)
    def _(h):
        cols = pl.ds(pl.multiple_of(h * HD, HD), HD)
        far = jnp.dot(
            unpick, ans_r[pl.ds(h * GRP, GRP)].reshape(rows, HD), preferred_element_type=jnp.float32
        )
        spread = jnp.zeros((slots, HD), jnp.float32)
        for g in range(GRP):
            spread = jnp.where(group_col == g, lse_r[h * GRP + g], spread)
        far_top = jnp.sum(jnp.where(lane == rank_col, spread, 0.0), axis=1, keepdims=True)
        top = own_top[h]
        joint = jnp.maximum(far_top, top)
        far_weight = jnp.exp2(far_top - joint)
        own_weight = jnp.exp2(top - joint)
        below = far_weight + own_weight * own_sum[h]
        mixed[:, cols] = (far_weight * far + own_weight * mixed[:, cols]) / below

    loads[4].wait()

    @pl.loop(0, slots // 16)
    def _(r):
        some = pl.ds(pl.multiple_of(r * 16, 16), 16)
        summed = x_ref[some, :].astype(jnp.float32) + mixed[some, :]
        tok[some, :] = norm_rows(summed, again_ref[...], ashift_ref[...]).astype(jnp.bfloat16)

    def y_copy(src, dst, send_sem, recv_sem, step):
        return pltpu.make_async_remote_copy(
            src_ref=src, dst_ref=dst, send_sem=send_sem, recv_sem=recv_sem,
            device_id=place(lax.rem(y + step + NY, NY), c, x, z), device_id_type=MESH,
        )

    def token(pos, part=None):
        return tok.at[pl.ds(pos * slots, slots)] if part is None else tok.at[
            pl.ds(pos * slots + part * (slots // 2), slots // 2)
        ]

    sent = [
        y_copy(token(0), token(2), t_send.at[0], t_recv.at[0], 1),
        y_copy(token(0), token(1), t_send.at[1], t_recv.at[1], -1),
    ]
    sent[0].start()
    sent[1].start()
    own_weights[0].wait()
    own_weights[1].wait()
    width = q_ref.shape[1]
    tile = 256
    per_tile = tile // 64

    def up(first, count):
        rows_ = pl.ds(first * slots, count * slots)

        @pl.loop(0, NC * DEV // per_tile)
        def _(n):
            cols = pl.ds(pl.multiple_of(n * tile, tile), tile)
            u = lax.dot_general(
                tok[rows_, :], wu[pl.ds(n * per_tile, per_tile)].reshape(tile, width), NT_DIMS,
                preferred_element_type=jnp.float32,
            )
            u = u + bias_all[:, cols]
            hidden[rows_, cols] = jax.nn.gelu(u, approximate=True).astype(jnp.bfloat16)

    def down(first, count):
        rows_ = pl.ds(first * slots, count * slots)

        @pl.loop(0, width // tile)
        def _(n):
            cols = pl.ds(pl.multiple_of(n * tile, tile), tile)
            total_acc[rows_, cols] = jnp.dot(
                hidden[rows_, :], wd[:, :, cols].reshape(NC * DEV * 64, tile),
                preferred_element_type=jnp.float32,
            )

    second_direct(1, 0)
    first_half(1)
    second_own(1, 3)
    for k in (1, 2, 3):
        second_half(0, k)
    cross_wait(0)
    second_direct(1, 1)
    second_direct(1, 2)
    up(0, 1)
    wait_bytes(token(2), t_recv.at[0])
    wait_bytes(token(1), t_recv.at[1])
    sent.append(y_copy(token(2, 0), token(3, 0), t_send.at[2], t_recv.at[2], 1))
    sent.append(y_copy(token(1, 1), token(3, 1), t_send.at[3], t_recv.at[3], -1))
    sent[2].start()
    sent[3].start()
    second_direct(1, 3)
    up(1, 2)
    wait_bytes(token(3, 0), t_recv.at[2])
    wait_bytes(token(3, 1), t_recv.at[3])
    up(3, 1)
    for k in range(4):
        second_half(1, k)
    cross_wait(1)
    down(3, 1)
    cut = width // 2

    def ship(src, dst, send_sem, recv_sem, side):
        sent.append(y_copy(src, dst, send_sem, recv_sem, 1 - 2 * side))
        sent[-1].start()

    for side in range(2):
        half_s[side] = total_acc[3 * slots :, side * cut : (side + 1) * cut].astype(jnp.bfloat16)
        ship(half_s.at[side], half_r.at[side], h_send.at[side], h_recv.at[side], side)
    down(1, 2)
    for side in range(2):
        at = slice((1 + side) * slots, (2 + side) * slots)
        rest = 1 - side
        part_s[side, 1] = total_acc[at, rest * cut : (rest + 1) * cut].astype(jnp.bfloat16)
        ship(part_s.at[side, 1], part_r.at[side, 1], p_send.at[side, 1], p_recv.at[side, 1], side)
    for side in range(2):
        at = slice((1 + side) * slots, (2 + side) * slots)
        wait_bytes(half_r.at[side], h_recv.at[side])
        joined = total_acc[at, side * cut : (side + 1) * cut] + half_r[side].astype(jnp.float32)
        part_s[side, 0] = joined.astype(jnp.bfloat16)
        ship(part_s.at[side, 0], part_r.at[side, 0], p_send.at[side, 0], p_recv.at[side, 0], side)
    down(0, 1)
    for kind in (1, 0):
        for side in range(2):
            wait_bytes(part_r.at[side, kind], p_recv.at[side, kind])

    @pl.loop(0, slots // 16)
    def _(r):
        some = pl.ds(pl.multiple_of(r * 16, 16), 16)
        total = total_acc[some, :] + tok[some, :].astype(jnp.float32) + dbias_ref[...]
        low = part_r[0, 0, some, :].astype(jnp.float32) + part_r[1, 1, some, :].astype(jnp.float32)
        high = part_r[0, 1, some, :].astype(jnp.float32) + part_r[1, 0, some, :].astype(jnp.float32)
        total = total + jnp.concatenate([low, high], axis=1)
        out_ref[some, :] = norm_rows(total, ogain_ref[...], oshift_ref[...]).astype(jnp.bfloat16)

    for copy in sent:
        copy.wait_send()
    wait_bytes(qs.at[pl.ds(0, GRP * DEV - 1)], q_send)
    wait_bytes(ans_s.at[pl.ds(0, GRP * DEV - 1)], a_send)
    wait_bytes(lse_s.at[pl.ds(0, GRP * DEV - 1)], l_send)
    wait_bytes(bias_r.at[pl.ds(0, NC * DEV - 1)], b_send)
    for ab in range(2):
        wait_bytes(weights[ab].at[pl.ds(0, NC * DEV - 1)], w_send.at[ab])


def vmem():
    return pl.BlockSpec(memory_space=pltpu.VMEM)


def on_device(
    queries, keys, values, layer_input, lengths, groups, prefix_keys, prefix_values,
    up_weight, up_bias, down_weight, down_bias, attn_gain, attn_shift, out_gain, out_shift,
):
    slots, width = queries.shape
    heads = width // HD
    plen = prefix_keys.shape[1]
    rows = GRP * CAP
    local = up_bias.shape[0]
    units = NC * DEV * local
    f32, bf16 = jnp.float32, jnp.bfloat16
    dma = pltpu.SemaphoreType.DMA
    smem = pl.BlockSpec(memory_space=pltpu.SMEM)
    anywhere = pl.BlockSpec(memory_space=pl.ANY)
    messages = pltpu.VMEM((GRP * DEV, CAP, HD), bf16)
    lines = pltpu.VMEM((GRP * DEV, 1, HD), f32)
    return pl.pallas_call(
        layer_kernel,
        out_shape=jax.ShapeDtypeStruct((slots, width), bf16),
        in_specs=[smem] * 2 + [vmem()] * 2 + [anywhere] * 7 + [vmem()] * 5,
        out_specs=vmem(),
        scratch_shapes=[
            pltpu.VMEM((slots, width), bf16),
            pltpu.VMEM((slots, width), bf16),
            pltpu.VMEM((slots, width), bf16),
            pltpu.VMEM((plen, HD), bf16),
            pltpu.VMEM((plen, HD), bf16),
            messages, messages, messages, messages, lines, lines,
            pltpu.VMEM((1, HD), f32),
            pltpu.VMEM((NC * DEV, 1, HD), f32),
            pltpu.VMEM((1, units), f32),
            pltpu.VMEM((rows, plen), f32),
            pltpu.VMEM((rows, plen), f32),
            pltpu.VMEM((rows, plen), bf16),
            pltpu.VMEM((rows, plen), bf16),
            pltpu.VMEM((rows, HD), f32),
            pltpu.VMEM((rows, HD), f32),
            pltpu.VMEM((2, rows, HD), f32),
            pltpu.VMEM((2, rows, HD), f32),
            pltpu.VMEM((slots, width), f32),
            pltpu.VMEM((heads, slots, 1), f32),
            pltpu.VMEM((heads, slots, 1), f32),
            pltpu.VMEM((NC * DEV, local, width), bf16),
            pltpu.VMEM((NC * DEV, local, width), bf16),
            pltpu.VMEM((NY * slots, width), bf16),
            pltpu.VMEM((NY * slots, units), bf16),
            pltpu.VMEM((NY * slots, width), f32),
            pltpu.VMEM((2, slots, width // 2), bf16),
            pltpu.VMEM((2, slots, width // 2), bf16),
            pltpu.VMEM((2, 2, slots, width // 2), bf16),
            pltpu.VMEM((2, 2, slots, width // 2), bf16),
            dma, dma((DEV,)), dma, dma, dma, dma, dma, dma, dma((4,)), dma((7,)),
            dma((2,)), dma((4, 5, 4)), dma((2,)), dma((4,)), dma((4,)), dma((2,)), dma((2,)), dma((2, 2)), dma((2, 2)),
        ],
        compiler_params=pltpu.CompilerParams(collective_id=0, has_side_effects=True, vmem_limit_bytes=LIMIT),
        name="layer",
    )(
        lengths, groups, queries, up_bias[None], keys, values, layer_input,
        prefix_keys[0], prefix_values[0], up_weight.T, down_weight,
        attn_gain[None], attn_shift[None], down_bias[None], out_gain[None], out_shift[None],
    )


def solution(mesh):
    fine = Mesh(mesh.devices.reshape(NY, NC, NX, NZ), ("y", "c", "x", "z"))
    grp, dev = ("y", "c"), ("x", "z")
    every = grp + dev
    token_rows = P(every, None)
    placed = (
        (token_rows,) * 6
        + (P(grp, None, dev),) * 2
        + (P(None, every), P(every), P(every, None))
        + (P(),) * 5
    )
    return jax.shard_map(on_device, mesh=fine, in_specs=placed, out_specs=token_rows, check_vma=False)
```

```python
import functools

import jax
import jax.numpy as jnp
from jax import lax
from jax.experimental import pallas as pl
from jax.experimental.pallas import tpu as pltpu
from jax.sharding import Mesh, PartitionSpec as P

HD = 128
NY, NC, NX, NZ = 4, 2, 4, 4
GRP, DEV = NY * NC, NX * NZ
CAP = 32
LOG2E = 1.4426950408889634
SCALE2 = HD**-0.5 * LOG2E
NORM_EPS = 1e-12
NEG = -1e30
MESH = pl.DeviceIdType.MESH
NT_DIMS = (((1,), (1,)), ((), ()))
LIMIT = 64 * 1024 * 1024 - 65536


def coordinates():
    return tuple(lax.axis_index(name) for name in ("y", "c", "x", "z"))


def place(y, c, x, z):
    return {"y": y, "c": c, "x": x, "z": z}


def plane_at(x, z, block):
    return lax.rem(x + block // NZ, NX), lax.rem(z + lax.rem(block, NZ), NZ)


def plane_back(x, z, block):
    return lax.rem(x + NX - block // NZ, NX), lax.rem(z + NZ - lax.rem(block, NZ), NZ)


def block_index(x, z, c):
    return z * (NC * NX) + c * NX + x


def wait_bytes(ref, sem):
    pltpu.make_async_copy(ref, ref, sem).wait()


def norm_rows(summed, gain, shift):
    mean = jnp.mean(summed, axis=-1, keepdims=True)
    centred = summed - mean
    spread = jnp.mean(centred * centred, axis=-1, keepdims=True)
    return centred * lax.rsqrt(spread + NORM_EPS) * gain + shift


def slot_tables(len_ref, grp_ref, shape, dim):
    slot = lax.broadcasted_iota(jnp.int32, shape, dim)
    start = jnp.int32(0)
    group = jnp.zeros(shape, jnp.int32)
    rank = jnp.zeros(shape, jnp.int32)
    for request in range(len_ref.shape[1]):
        length = len_ref[0, request]
        inside = (slot >= start) & (slot < start + length)
        group = jnp.where(inside, grp_ref[0, request], group)
        rank = jnp.where(inside, slot - start, rank)
        start = start + length
    return group, rank


def layer_kernel(
    len_ref, grp_ref, q_ref, bias_ref, k_in, v_in, x_in, pk_in, pv_in, up_in, down_in,
    again_ref, ashift_ref, dbias_ref, ogain_ref, oshift_ref,
    out_ref,
    k_ref, v_ref, x_ref, pk_ref, pv_ref,
    qs, qr, ans_s, ans_r, lse_s, lse_r, bias_s, bias_r, bias_all,
    s0, s1, p0, p1, acc, peak, tops, sums, mixed, own_top, own_sum,
    wu, wd, tok, hidden, total_acc, half_s, half_r, part_s, part_r,
    q_send, q_recv, a_send, a_recv, l_send, l_recv, b_send, b_recv, self_sem, in_sem,
    w_send, w_recv, w_cross, t_send, t_recv, h_send, h_recv, p_send, p_recv,
):
    y, c, x, z = coordinates()
    me_g = y * NC + c
    me_d = x * NZ + z
    slots = q_ref.shape[0]
    heads = q_ref.shape[1] // HD
    s_bufs, p_bufs = (s0, s1), (p0, p1)
    rows = GRP * CAP
    plen = pk_ref.shape[0]

    def group_at(k):
        g = lax.rem(me_g + k, GRP)
        return g, g // NC, lax.rem(g, NC)

    loads = [
        pltpu.make_async_copy(src, dst, in_sem.at[n])
        for n, (src, dst) in enumerate(
            ((k_in, k_ref), (v_in, v_ref), (pk_in, pk_ref), (pv_in, pv_ref), (x_in, x_ref))
        )
    ]
    for load in loads:
        load.start()
    barrier = pltpu.get_barrier_semaphore()

    def greet(block, k):
        tx, tz = plane_at(x, z, block)
        _, ty, tc = group_at(k)
        pl.semaphore_signal(barrier, inc=1, device_id=place(ty, tc, tx, tz), device_id_type=MESH)

    for k in range(1, GRP):
        greet(0, k)

    @pl.loop(1, DEV)
    def _(block):
        for k in range(GRP):
            greet(block, k)

    group_row, rank_row = slot_tables(len_ref, grp_ref, (1, slots), 1)
    pick = lax.broadcasted_iota(jnp.int32, (rows, slots), 0) == group_row * CAP + rank_row
    pick = pick.astype(jnp.float32).astype(jnp.bfloat16)
    line = bias_ref[...].astype(jnp.float32)
    line = jnp.concatenate([line, line], axis=1)
    side = lax.broadcasted_iota(jnp.int32, line.shape, 1) // (HD // 2)
    bias_s[...] = jnp.where(side == lax.rem(x, 2), line, 0.0)
    for d in range(heads):
        packed = jnp.dot(pick, q_ref[:, d * HD : (d + 1) * HD], preferred_element_type=jnp.float32)
        packed = packed.astype(jnp.bfloat16).reshape(GRP, CAP, HD)
        for g in range(GRP):
            qs[g * DEV + d] = packed[g]
    pl.semaphore_wait(barrier, GRP * DEV - 1)

    weights = (wu, wd)
    sources = (up_in, down_in)
    ring_steps = (0, -1, 1, 2)
    strip = up_in.shape[0] // 2

    def block_of(q, r1, r2):
        rx, rz = (r1, r2) if q % 2 == 0 else (r2, r1)
        return block_index(lax.rem(x + rx + NX, NX), lax.rem(z + rz + NZ, NZ), c)

    def along(q, axis, step):
        if (q + axis) % 2 == 0:
            return place(y, c, lax.rem(x + step + NX, NX), z)
        return place(y, c, x, lax.rem(z + step + NZ, NZ))

    partner = place(y, 1 - c, x, z)

    def strip_of(block, q, part):
        first = (q % 2) * strip
        if part is None:
            return block.at[pl.ds(first, strip)]
        return block.at[pl.ds(first + part * (strip // 2), strip // 2)]

    def weight_refs(q, r1, r2, part):
        dst = strip_of(weights[q // 2].at[block_of(q, r1, r2)], q, part)
        src = strip_of(sources[q // 2], q, part) if (r1 == 0 and r2 == 0) else dst
        return src, dst

    def weight_send(q, r1, r2, part, axis, step, phase, kind):
        src, dst = weight_refs(q, r1, r2, part)
        pltpu.make_async_remote_copy(
            src_ref=src, dst_ref=dst, send_sem=w_send.at[q // 2], recv_sem=w_recv.at[q, phase, kind],
            device_id=along(q, axis, step), device_id_type=MESH,
        ).start()

    def weight_cross(q, r1, r2):
        src, dst = weight_refs(q, r1, r2, None)
        pltpu.make_async_remote_copy(
            src_ref=src, dst_ref=dst, send_sem=w_send.at[q // 2], recv_sem=w_cross.at[q // 2],
            device_id=partner, device_id_type=MESH,
        ).start()

    def weight_wait(q, phase, kind):
        size = strip if kind < 2 else strip // 2
        wait_bytes(weights[q // 2].at[0, pl.ds(0, size)], w_recv.at[q, phase, kind])

    def both(tensor):
        return (2 * tensor, 2 * tensor + 1)

    def first_own(tensor):
        for q in both(tensor):
            weight_send(q, 0, 0, None, 0, 1, 0, 0)
            weight_send(q, 0, 0, None, 0, -1, 0, 1)
            weight_cross(q, 0, 0)

    def first_direct(tensor):
        for q in both(tensor):
            weight_wait(q, 0, 0)
            weight_send(q, -1, 0, 0, 0, 1, 0, 2)
            weight_wait(q, 0, 1)
            weight_send(q, 1, 0, 1, 0, -1, 0, 3)
            weight_cross(q, -1, 0)
            weight_cross(q, 1, 0)

    def first_half(tensor):
        for q in both(tensor):
            weight_wait(q, 0, 2)
            weight_wait(q, 0, 3)
            weight_cross(q, 2, 0)

    def second_own(tensor, k):
        for q in both(tensor):
            weight_send(q, ring_steps[k], 0, None, 1, 1, 1 + k, 0)
            weight_send(q, ring_steps[k], 0, None, 1, -1, 1 + k, 1)

    def second_direct(tensor, k):
        r1 = ring_steps[k]
        for q in both(tensor):
            weight_wait(q, 1 + k, 0)
            weight_send(q, r1, -1, 0, 1, 1, 1 + k, 2)
            weight_wait(q, 1 + k, 1)
            weight_send(q, r1, 1, 1, 1, -1, 1 + k, 3)
            weight_cross(q, r1, -1)
            weight_cross(q, r1, 1)

    def second_half(tensor, k):
        for q in both(tensor):
            weight_wait(q, 1 + k, 2)
            weight_wait(q, 1 + k, 3)
            weight_cross(q, ring_steps[k], 2)

    def cross_wait(tensor):
        wait_bytes(weights[tensor].at[pl.ds(0, DEV)], w_cross.at[tensor])

    own_weights = [
        pltpu.make_async_copy(sources[ab], weights[ab].at[block_index(x, z, c)], in_sem.at[5 + ab])
        for ab in range(2)
    ]

    def send_query(block, k):
        tx, tz = plane_at(x, z, block)
        g, ty, tc = group_at(k)
        pltpu.make_async_remote_copy(
            src_ref=qs.at[g * DEV + tx * NZ + tz],
            dst_ref=qr.at[block * GRP + me_g],
            send_sem=q_send,
            recv_sem=q_recv.at[block],
            device_id=place(ty, tc, tx, tz),
            device_id_type=MESH,
        ).start()

    own_query = pltpu.make_async_copy(qs.at[me_g * DEV + me_d], qr.at[me_g], self_sem.at[0])
    own_query.start()
    for k in range(1, GRP):
        send_query(0, k)

    @pl.loop(1, DEV)
    def _(block):
        for k in range(GRP):
            send_query(block, k)

    for k in range(1, NC * DEV):
        tc = lax.rem(c + k // DEV, NC)
        tx, tz = plane_at(x, z, k % DEV)
        pltpu.make_async_remote_copy(
            src_ref=bias_s,
            dst_ref=bias_r.at[block_index(x, z, c)],
            send_sem=b_send,
            recv_sem=b_recv,
            device_id=place(y, tc, tx, tz),
            device_id_type=MESH,
        ).start()
    own_bias = pltpu.make_async_copy(bias_s, bias_r.at[block_index(x, z, c)], self_sem.at[3])
    own_bias.start()
    own_weights[0].start()
    own_weights[1].start()
    first_own(0)
    second_own(0, 0)
    loads[0].wait()
    loads[1].wait()

    group_col, rank_col = slot_tables(len_ref, grp_ref, (slots, 1), 0)
    visible = (group_col == group_row) & (
        lax.broadcasted_iota(jnp.int32, (slots, slots), 1)
        <= lax.broadcasted_iota(jnp.int32, (slots, slots), 0)
    )

    @pl.loop(0, heads)
    def _(h):
        cols = pl.ds(pl.multiple_of(h * HD, HD), HD)
        s = lax.dot_general(q_ref[:, cols], k_ref[:, cols], NT_DIMS, preferred_element_type=jnp.float32)
        s = jnp.where(visible, s * SCALE2, NEG)
        top = jnp.max(s, axis=1, keepdims=True)
        w = jnp.where(visible, jnp.exp2(s - top), 0.0)
        own_top[h] = top
        own_sum[h] = jnp.sum(w, axis=1, keepdims=True)
        mixed[:, cols] = jnp.dot(w.astype(jnp.bfloat16), v_ref[:, cols], preferred_element_type=jnp.float32)

    def answer_back(block, k):
        tx, tz = plane_back(x, z, block)
        g, ty, tc = group_at(k)
        where = place(ty, tc, tx, tz)
        pltpu.make_async_remote_copy(
            src_ref=ans_s.at[block * GRP + g],
            dst_ref=ans_r.at[me_d * GRP + me_g],
            send_sem=a_send, recv_sem=a_recv, device_id=where, device_id_type=MESH,
        ).start()
        pltpu.make_async_remote_copy(
            src_ref=lse_s.at[block * GRP + g],
            dst_ref=lse_r.at[me_d * GRP + me_g],
            send_sem=l_send, recv_sem=l_recv, device_id=where, device_id_type=MESH,
        ).start()

    steps = 4
    span = plen // steps
    part = rows // steps

    def stage(i, parity, scoring, weighing, mixing, first=False):
        other = 1 - parity
        if scoring:
            if first:
                wait_bytes(qr.at[pl.ds(0, GRP - 1)], q_recv.at[0])
                own_query.wait()
            else:
                wait_bytes(qr.at[pl.ds(i * GRP, GRP)], q_recv.at[i])
            peak[...] = jnp.full_like(peak, NEG)
        if mixing:
            acc[...] = jnp.zeros_like(acc)

        @pl.loop(0, steps)
        def _(j):
            keys = pl.ds(pl.multiple_of(j * span, span), span)
            if scoring:
                block = qr[pl.ds(i * GRP, GRP)].reshape(rows, HD)
                s = lax.dot_general(block, pk_ref[keys, :], NT_DIMS, preferred_element_type=jnp.float32)
                s_bufs[parity][:, keys] = s
                high = s[:, :HD]
                for t in range(1, span // HD):
                    high = jnp.maximum(high, s[:, t * HD : (t + 1) * HD])
                peak[...] = jnp.maximum(peak[...], high)
            if weighing:
                some = pl.ds(pl.multiple_of(j * part, part), part)
                top = tops[other, some, :]
                total = jnp.zeros((part, HD), jnp.float32)
                for t in range(plen // HD):
                    cols = slice(t * HD, (t + 1) * HD)
                    w = jnp.exp2(s_bufs[other][some, cols] * SCALE2 - top)
                    total = total + w
                    p_bufs[other][some, cols] = w.astype(jnp.bfloat16)
                sums[other, some, :] = total
            if mixing:
                acc[...] += jnp.dot(p_bufs[parity][:, keys], pv_ref[keys, :], preferred_element_type=jnp.float32)

        if mixing:
            done = i - 2
            total = jnp.sum(sums[parity], axis=1, keepdims=True)
            answer = (acc[...] / total).astype(jnp.bfloat16).reshape(GRP, CAP, HD)
            spread = (tops[parity] + jnp.log(total) * LOG2E).reshape(GRP, CAP, HD)
            diagonal = lax.broadcasted_iota(jnp.int32, (GRP, CAP, HD), 1) == lax.broadcasted_iota(
                jnp.int32, (GRP, CAP, HD), 2
            )
            lines = jnp.sum(jnp.where(diagonal, spread, 0.0), axis=1)
            for g in range(GRP):
                ans_s[done * GRP + g] = answer[g]
                lse_s[done * GRP + g] = lines[g : g + 1]
        if scoring:
            tops[parity] = jnp.broadcast_to(jnp.max(peak[...], axis=1, keepdims=True) * SCALE2, (rows, HD))

    def send_back(done):
        for k in range(GRP):
            answer_back(done, k)

    loads[2].wait()
    loads[3].wait()
    stage(0, 0, True, False, False, first=True)
    stage(1, 1, True, True, False)
    stage(2, 0, True, True, True)
    own_answer = pltpu.make_async_copy(ans_s.at[me_g], ans_r.at[me_d * GRP + me_g], self_sem.at[1])
    own_lse = pltpu.make_async_copy(lse_s.at[me_g], lse_r.at[me_d * GRP + me_g], self_sem.at[2])
    own_answer.start()
    own_lse.start()
    for k in range(1, GRP):
        answer_back(0, k)
    stage(3, 1, True, True, True)
    send_back(1)

    def stage_pairs(first_pair, last_pair):
        @pl.loop(first_pair, last_pair)
        def _(pair):
            stage(2 * pair, 0, True, True, True)
            send_back(2 * pair - 2)
            stage(2 * pair + 1, 1, True, True, True)
            send_back(2 * pair - 1)

    stage_pairs(2, 4)
    first_direct(0)
    second_own(0, 1)
    stage_pairs(4, 6)
    second_direct(0, 0)
    first_half(0)
    second_own(0, 2)
    stage_pairs(6, 8)
    stage(DEV, 0, False, True, True)
    send_back(DEV - 2)
    stage(DEV + 1, 1, False, False, True)
    send_back(DEV - 1)

    own_bias.wait()
    wait_bytes(bias_r.at[pl.ds(0, NC * DEV - 1)], b_recv)
    for e in range(NC * DEV // 2):
        bias_all[:, e * HD : (e + 1) * HD] = bias_r[2 * e] + bias_r[2 * e + 1]

    second_direct(0, 1)
    second_direct(0, 2)
    second_own(0, 3)
    first_own(1)
    second_own(1, 0)
    second_half(0, 0)
    own_answer.wait()
    own_lse.wait()
    wait_bytes(ans_r.at[pl.ds(0, GRP * DEV - 1)], a_recv)
    wait_bytes(lse_r.at[pl.ds(0, GRP * DEV - 1)], l_recv)
    unpick = lax.broadcasted_iota(jnp.int32, (slots, rows), 1) == group_col * CAP + rank_col
    unpick = unpick.astype(jnp.float32).astype(jnp.bfloat16)
    lane = lax.broadcasted_iota(jnp.int32, (slots, HD), 1)

    @pl.loop(0, heads)
    def _(h):
        cols = pl.ds(pl.multiple_of(h * HD, HD), HD)
        far = jnp.dot(
            unpick, ans_r[pl.ds(h * GRP, GRP)].reshape(rows, HD), preferred_element_type=jnp.float32
        )
        spread = jnp.zeros((slots, HD), jnp.float32)
        for g in range(GRP):
            spread = jnp.where(group_col == g, lse_r[h * GRP + g], spread)
        far_top = jnp.sum(jnp.where(lane == rank_col, spread, 0.0), axis=1, keepdims=True)
        top = own_top[h]
        joint = jnp.maximum(far_top, top)
        far_weight = jnp.exp2(far_top - joint)
        own_weight = jnp.exp2(top - joint)
        below = far_weight + own_weight * own_sum[h]
        mixed[:, cols] = (far_weight * far + own_weight * mixed[:, cols]) / below

    second_direct(0, 3)
    first_direct(1)
    second_own(1, 1)
    second_own(1, 2)
    loads[4].wait()

    @pl.loop(0, slots // 16)
    def _(r):
        some = pl.ds(pl.multiple_of(r * 16, 16), 16)
        summed = x_ref[some, :].astype(jnp.float32) + mixed[some, :]
        tok[some, :] = norm_rows(summed, again_ref[...], ashift_ref[...]).astype(jnp.bfloat16)

    def y_copy(src, dst, send_sem, recv_sem, step):
        return pltpu.make_async_remote_copy(
            src_ref=src, dst_ref=dst, send_sem=send_sem, recv_sem=recv_sem,
            device_id=place(lax.rem(y + step + NY, NY), c, x, z), device_id_type=MESH,
        )

    def token(pos, part=None):
        return tok.at[pl.ds(pos * slots, slots)] if part is None else tok.at[
            pl.ds(pos * slots + part * (slots // 2), slots // 2)
        ]

    sent = []
    for n, (part, target, step) in enumerate(((0, 2, 1), (1, 1, -1), (1, 2, 1), (0, 1, -1))):
        sent.append(y_copy(token(0, part), token(target, part), t_send.at[n], t_recv.at[n], step))
        sent[-1].start()
    own_weights[0].wait()
    own_weights[1].wait()
    width = q_ref.shape[1]
    tile = 256
    per_tile = tile // 64

    def up(first, count):
        rows_ = pl.ds(first * slots, count * slots)

        @pl.loop(0, NC * DEV // per_tile)
        def _(n):
            cols = pl.ds(pl.multiple_of(n * tile, tile), tile)
            u = lax.dot_general(
                tok[rows_, :], wu[pl.ds(n * per_tile, per_tile)].reshape(tile, width), NT_DIMS,
                preferred_element_type=jnp.float32,
            )
            u = u + bias_all[:, cols]
            hidden[rows_, cols] = jax.nn.gelu(u, approximate=True).astype(jnp.bfloat16)

    def down(first, count, low, high):
        rows_ = pl.ds(first * slots, count * slots)

        @pl.loop(low * (width // tile // 2), high * (width // tile // 2))
        def _(n):
            cols = pl.ds(pl.multiple_of(n * tile, tile), tile)
            total_acc[rows_, cols] = jnp.dot(
                hidden[rows_, :], wd[:, :, cols].reshape(NC * DEV * 64, tile),
                preferred_element_type=jnp.float32,
            )

    second_direct(1, 0)
    first_half(1)
    second_own(1, 3)
    for k in (1, 2, 3):
        second_half(0, k)
    cross_wait(0)
    for n, (part, origin, step) in enumerate(((0, 2, 1), (1, 1, -1))):
        wait_bytes(token(origin, part), t_recv.at[n])
        sent.append(y_copy(token(origin, part), token(3, part), t_send.at[4 + n], t_recv.at[4 + n], step))
        sent[-1].start()
    second_direct(1, 1)
    second_direct(1, 2)
    up(0, 1)
    wait_bytes(token(2, 1), t_recv.at[2])
    wait_bytes(token(1, 0), t_recv.at[3])
    second_direct(1, 3)
    up(1, 2)
    wait_bytes(token(3, 0), t_recv.at[4])
    wait_bytes(token(3, 1), t_recv.at[5])
    up(3, 1)
    for k in range(4):
        second_half(1, k)
    cross_wait(1)
    cut = width // 2

    def ship(src, dst, send_sem, recv_sem, side):
        sent.append(y_copy(src, dst, send_sem, recv_sem, 1 - 2 * side))
        sent[-1].start()

    for side in range(2):
        down(3, 1, side, side + 1)
        half_s[side] = total_acc[3 * slots :, side * cut : (side + 1) * cut].astype(jnp.bfloat16)
        ship(half_s.at[side], half_r.at[side], h_send.at[side], h_recv.at[side], side)
    for rest in range(2):
        side = 1 - rest
        at = slice((1 + side) * slots, (2 + side) * slots)
        down(1, 2, rest, rest + 1)
        part_s[side, 1] = total_acc[at, rest * cut : (rest + 1) * cut].astype(jnp.bfloat16)
        ship(part_s.at[side, 1], part_r.at[side, 1], p_send.at[side, 1], p_recv.at[side, 1], side)
    for side in range(2):
        at = slice((1 + side) * slots, (2 + side) * slots)
        wait_bytes(half_r.at[side], h_recv.at[side])
        joined = total_acc[at, side * cut : (side + 1) * cut] + half_r[side].astype(jnp.float32)
        part_s[side, 0] = joined.astype(jnp.bfloat16)
        ship(part_s.at[side, 0], part_r.at[side, 0], p_send.at[side, 0], p_recv.at[side, 0], side)
    down(0, 1, 0, 2)
    for kind in (1, 0):
        for side in range(2):
            wait_bytes(part_r.at[side, kind], p_recv.at[side, kind])

    @pl.loop(0, slots // 16)
    def _(r):
        some = pl.ds(pl.multiple_of(r * 16, 16), 16)
        total = total_acc[some, :] + tok[some, :].astype(jnp.float32) + dbias_ref[...]
        low = part_r[0, 0, some, :].astype(jnp.float32) + part_r[1, 1, some, :].astype(jnp.float32)
        high = part_r[0, 1, some, :].astype(jnp.float32) + part_r[1, 0, some, :].astype(jnp.float32)
        total = total + jnp.concatenate([low, high], axis=1)
        out_ref[some, :] = norm_rows(total, ogain_ref[...], oshift_ref[...]).astype(jnp.bfloat16)

    for copy in sent:
        copy.wait_send()
    wait_bytes(qs.at[pl.ds(0, GRP * DEV - 1)], q_send)
    wait_bytes(ans_s.at[pl.ds(0, GRP * DEV - 1)], a_send)
    wait_bytes(lse_s.at[pl.ds(0, GRP * DEV - 1)], l_send)
    wait_bytes(bias_r.at[pl.ds(0, NC * DEV - 1)], b_send)
    for ab in range(2):
        wait_bytes(weights[ab].at[pl.ds(0, NC * DEV - 1)], w_send.at[ab])


def vmem():
    return pl.BlockSpec(memory_space=pltpu.VMEM)


def on_device(
    queries, keys, values, layer_input, lengths, groups, prefix_keys, prefix_values,
    up_weight, up_bias, down_weight, down_bias, attn_gain, attn_shift, out_gain, out_shift,
):
    slots, width = queries.shape
    heads = width // HD
    plen = prefix_keys.shape[1]
    rows = GRP * CAP
    local = up_bias.shape[0]
    units = NC * DEV * local
    f32, bf16 = jnp.float32, jnp.bfloat16
    dma = pltpu.SemaphoreType.DMA
    smem = pl.BlockSpec(memory_space=pltpu.SMEM)
    anywhere = pl.BlockSpec(memory_space=pl.ANY)
    messages = pltpu.VMEM((GRP * DEV, CAP, HD), bf16)
    lines = pltpu.VMEM((GRP * DEV, 1, HD), f32)
    return pl.pallas_call(
        layer_kernel,
        out_shape=jax.ShapeDtypeStruct((slots, width), bf16),
        in_specs=[smem] * 2 + [vmem()] * 2 + [anywhere] * 7 + [vmem()] * 5,
        out_specs=vmem(),
        scratch_shapes=[
            pltpu.VMEM((slots, width), bf16),
            pltpu.VMEM((slots, width), bf16),
            pltpu.VMEM((slots, width), bf16),
            pltpu.VMEM((plen, HD), bf16),
            pltpu.VMEM((plen, HD), bf16),
            messages, messages, messages, messages, lines, lines,
            pltpu.VMEM((1, HD), f32),
            pltpu.VMEM((NC * DEV, 1, HD), f32),
            pltpu.VMEM((1, units), f32),
            pltpu.VMEM((rows, plen), f32),
            pltpu.VMEM((rows, plen), f32),
            pltpu.VMEM((rows, plen), bf16),
            pltpu.VMEM((rows, plen), bf16),
            pltpu.VMEM((rows, HD), f32),
            pltpu.VMEM((rows, HD), f32),
            pltpu.VMEM((2, rows, HD), f32),
            pltpu.VMEM((2, rows, HD), f32),
            pltpu.VMEM((slots, width), f32),
            pltpu.VMEM((heads, slots, 1), f32),
            pltpu.VMEM((heads, slots, 1), f32),
            pltpu.VMEM((NC * DEV, local, width), bf16),
            pltpu.VMEM((NC * DEV, local, width), bf16),
            pltpu.VMEM((NY * slots, width), bf16),
            pltpu.VMEM((NY * slots, units), bf16),
            pltpu.VMEM((NY * slots, width), f32),
            pltpu.VMEM((2, slots, width // 2), bf16),
            pltpu.VMEM((2, slots, width // 2), bf16),
            pltpu.VMEM((2, 2, slots, width // 2), bf16),
            pltpu.VMEM((2, 2, slots, width // 2), bf16),
            dma, dma((DEV,)), dma, dma, dma, dma, dma, dma, dma((4,)), dma((7,)),
            dma((2,)), dma((4, 5, 4)), dma((2,)), dma((6,)), dma((6,)), dma((2,)), dma((2,)), dma((2, 2)), dma((2, 2)),
        ],
        compiler_params=pltpu.CompilerParams(collective_id=0, has_side_effects=True, vmem_limit_bytes=LIMIT),
        name="layer",
    )(
        lengths, groups, queries, up_bias[None], keys, values, layer_input,
        prefix_keys[0], prefix_values[0], up_weight.T, down_weight,
        attn_gain[None], attn_shift[None], down_bias[None], out_gain[None], out_shift[None],
    )


def solution(mesh):
    fine = Mesh(mesh.devices.reshape(NY, NC, NX, NZ), ("y", "c", "x", "z"))
    grp, dev = ("y", "c"), ("x", "z")
    every = grp + dev
    token_rows = P(every, None)
    placed = (
        (token_rows,) * 6
        + (P(grp, None, dev),) * 2
        + (P(None, every), P(every), P(every, None))
        + (P(),) * 5
    )
    return jax.shard_map(on_device, mesh=fine, in_specs=placed, out_specs=token_rows, check_vma=False)
```

```python
import functools

import jax
import jax.numpy as jnp
from jax import lax
from jax.experimental import pallas as pl
from jax.experimental.pallas import tpu as pltpu
from jax.sharding import Mesh, PartitionSpec as P

HD = 128
NY, NC, NX, NZ = 4, 2, 4, 4
GRP, DEV = NY * NC, NX * NZ
CAP = 32
LOG2E = 1.4426950408889634
SCALE2 = HD**-0.5 * LOG2E
NORM_EPS = 1e-12
NEG = -1e30
MESH = pl.DeviceIdType.MESH
NT_DIMS = (((1,), (1,)), ((), ()))
LIMIT = 64 * 1024 * 1024 - 65536


def coordinates():
    return tuple(lax.axis_index(name) for name in ("y", "c", "x", "z"))


def place(y, c, x, z):
    return {"y": y, "c": c, "x": x, "z": z}


def plane_at(x, z, block):
    return lax.rem(x + block // NZ, NX), lax.rem(z + lax.rem(block, NZ), NZ)


def plane_back(x, z, block):
    return lax.rem(x + NX - block // NZ, NX), lax.rem(z + NZ - lax.rem(block, NZ), NZ)


def block_index(x, z, c):
    return z * (NC * NX) + c * NX + x


def wait_bytes(ref, sem):
    pltpu.make_async_copy(ref, ref, sem).wait()


def norm_rows(summed, gain, shift):
    mean = jnp.mean(summed, axis=-1, keepdims=True)
    centred = summed - mean
    spread = jnp.mean(centred * centred, axis=-1, keepdims=True)
    return centred * lax.rsqrt(spread + NORM_EPS) * gain + shift


def slot_tables(len_ref, grp_ref, shape, dim):
    slot = lax.broadcasted_iota(jnp.int32, shape, dim)
    start = jnp.int32(0)
    group = jnp.zeros(shape, jnp.int32)
    rank = jnp.zeros(shape, jnp.int32)
    for request in range(len_ref.shape[1]):
        length = len_ref[0, request]
        inside = (slot >= start) & (slot < start + length)
        group = jnp.where(inside, grp_ref[0, request], group)
        rank = jnp.where(inside, slot - start, rank)
        start = start + length
    return group, rank


def layer_kernel(
    len_ref, grp_ref, q_ref, bias_ref, k_in, v_in, x_in, pk_in, pv_in, up_in, down_in,
    again_ref, ashift_ref, dbias_ref, ogain_ref, oshift_ref,
    out_ref,
    k_ref, v_ref, x_ref, pk_ref, pv_ref,
    qs, qr, ans_s, ans_r, lse_s, lse_r, bias_s, bias_r, bias_all,
    s0, s1, p0, p1, acc, peak, tops, sums, mixed, own_top, own_sum,
    wu, wd, tok, hidden, total_acc, half_s, half_r, part_s, part_r,
    q_send, q_recv, a_send, a_recv, l_send, l_recv, b_send, b_recv, self_sem, in_sem,
    w_send, w_recv, w_cross, t_send, t_recv, h_send, h_recv, p_send, p_recv,
):
    y, c, x, z = coordinates()
    me_g = y * NC + c
    me_d = x * NZ + z
    slots = q_ref.shape[0]
    heads = q_ref.shape[1] // HD
    s_bufs, p_bufs = (s0, s1), (p0, p1)
    rows = GRP * CAP
    plen = pk_ref.shape[0]

    def group_at(k):
        g = lax.rem(me_g + k, GRP)
        return g, g // NC, lax.rem(g, NC)

    loads = [
        pltpu.make_async_copy(src, dst, in_sem.at[n])
        for n, (src, dst) in enumerate(
            ((k_in, k_ref), (v_in, v_ref), (pk_in, pk_ref), (pv_in, pv_ref), (x_in, x_ref))
        )
    ]
    for load in loads:
        load.start()
    barrier = pltpu.get_barrier_semaphore()

    def greet(block, k):
        tx, tz = plane_at(x, z, block)
        _, ty, tc = group_at(k)
        pl.semaphore_signal(barrier, inc=1, device_id=place(ty, tc, tx, tz), device_id_type=MESH)

    for k in range(1, GRP):
        greet(0, k)

    @pl.loop(1, DEV)
    def _(block):
        for k in range(GRP):
            greet(block, k)

    group_row, rank_row = slot_tables(len_ref, grp_ref, (1, slots), 1)
    pick = lax.broadcasted_iota(jnp.int32, (rows, slots), 0) == group_row * CAP + rank_row
    pick = pick.astype(jnp.float32).astype(jnp.bfloat16)
    line = bias_ref[...].astype(jnp.float32)
    line = jnp.concatenate([line, line], axis=1)
    side = lax.broadcasted_iota(jnp.int32, line.shape, 1) // (HD // 2)
    bias_s[...] = jnp.where(side == lax.rem(x, 2), line, 0.0)
    for d in range(heads):
        packed = jnp.dot(pick, q_ref[:, d * HD : (d + 1) * HD], preferred_element_type=jnp.float32)
        packed = packed.astype(jnp.bfloat16).reshape(GRP, CAP, HD)
        for g in range(GRP):
            qs[g * DEV + d] = packed[g]
    pl.semaphore_wait(barrier, GRP * DEV - 1)

    weights = (wu, wd)
    sources = (up_in, down_in)
    ring_steps = (0, -1, 1, 2)
    strip = up_in.shape[0] // 2

    def block_of(q, r1, r2):
        rx, rz = (r1, r2) if q % 2 == 0 else (r2, r1)
        return block_index(lax.rem(x + rx + NX, NX), lax.rem(z + rz + NZ, NZ), c)

    def along(q, axis, step):
        if (q + axis) % 2 == 0:
            return place(y, c, lax.rem(x + step + NX, NX), z)
        return place(y, c, x, lax.rem(z + step + NZ, NZ))

    partner = place(y, 1 - c, x, z)

    def strip_of(block, q, part):
        first = (q % 2) * strip
        if part is None:
            return block.at[pl.ds(first, strip)]
        return block.at[pl.ds(first + part * (strip // 2), strip // 2)]

    def weight_refs(q, r1, r2, part):
        dst = strip_of(weights[q // 2].at[block_of(q, r1, r2)], q, part)
        src = strip_of(sources[q // 2], q, part) if (r1 == 0 and r2 == 0) else dst
        return src, dst

    def weight_send(q, r1, r2, part, axis, step, phase, kind):
        src, dst = weight_refs(q, r1, r2, part)
        pltpu.make_async_remote_copy(
            src_ref=src, dst_ref=dst, send_sem=w_send.at[q // 2], recv_sem=w_recv.at[q, phase, kind],
            device_id=along(q, axis, step), device_id_type=MESH,
        ).start()

    def weight_cross(q, r1, r2):
        src, dst = weight_refs(q, r1, r2, None)
        pltpu.make_async_remote_copy(
            src_ref=src, dst_ref=dst, send_sem=w_send.at[q // 2], recv_sem=w_cross.at[q // 2],
            device_id=partner, device_id_type=MESH,
        ).start()

    def weight_wait(q, phase, kind):
        size = strip if kind < 2 else strip // 2
        wait_bytes(weights[q // 2].at[0, pl.ds(0, size)], w_recv.at[q, phase, kind])

    def both(tensor):
        return (2 * tensor, 2 * tensor + 1)

    def first_own(tensor):
        for q in both(tensor):
            weight_send(q, 0, 0, None, 0, 1, 0, 0)
            weight_send(q, 0, 0, None, 0, -1, 0, 1)
            weight_cross(q, 0, 0)

    def first_direct(tensor):
        for q in both(tensor):
            weight_wait(q, 0, 0)
            weight_send(q, -1, 0, 0, 0, 1, 0, 2)
            weight_wait(q, 0, 1)
            weight_send(q, 1, 0, 1, 0, -1, 0, 3)
            weight_cross(q, -1, 0)
            weight_cross(q, 1, 0)

    def first_half(tensor):
        for q in both(tensor):
            weight_wait(q, 0, 2)
            weight_wait(q, 0, 3)
            weight_cross(q, 2, 0)

    def second_own(tensor, k):
        for q in both(tensor):
            weight_send(q, ring_steps[k], 0, None, 1, 1, 1 + k, 0)
            weight_send(q, ring_steps[k], 0, None, 1, -1, 1 + k, 1)

    def second_direct(tensor, k):
        r1 = ring_steps[k]
        for q in both(tensor):
            weight_wait(q, 1 + k, 0)
            weight_send(q, r1, -1, 0, 1, 1, 1 + k, 2)
            weight_wait(q, 1 + k, 1)
            weight_send(q, r1, 1, 1, 1, -1, 1 + k, 3)
            weight_cross(q, r1, -1)
            weight_cross(q, r1, 1)

    def second_half(tensor, k):
        for q in both(tensor):
            weight_wait(q, 1 + k, 2)
            weight_wait(q, 1 + k, 3)
            weight_cross(q, ring_steps[k], 2)

    def cross_wait(tensor):
        wait_bytes(weights[tensor].at[pl.ds(0, DEV)], w_cross.at[tensor])

    own_weights = [
        pltpu.make_async_copy(sources[ab], weights[ab].at[block_index(x, z, c)], in_sem.at[5 + ab])
        for ab in range(2)
    ]

    def send_query(block, k):
        tx, tz = plane_at(x, z, block)
        g, ty, tc = group_at(k)
        pltpu.make_async_remote_copy(
            src_ref=qs.at[g * DEV + tx * NZ + tz],
            dst_ref=qr.at[block * GRP + me_g],
            send_sem=q_send,
            recv_sem=q_recv.at[block],
            device_id=place(ty, tc, tx, tz),
            device_id_type=MESH,
        ).start()

    own_query = pltpu.make_async_copy(qs.at[me_g * DEV + me_d], qr.at[me_g], self_sem.at[0])
    own_query.start()
    for k in range(1, GRP):
        send_query(0, k)

    @pl.loop(1, DEV)
    def _(block):
        for k in range(GRP):
            send_query(block, k)

    for k in range(1, NC * DEV):
        tc = lax.rem(c + k // DEV, NC)
        tx, tz = plane_at(x, z, k % DEV)
        pltpu.make_async_remote_copy(
            src_ref=bias_s,
            dst_ref=bias_r.at[block_index(x, z, c)],
            send_sem=b_send,
            recv_sem=b_recv,
            device_id=place(y, tc, tx, tz),
            device_id_type=MESH,
        ).start()
    own_bias = pltpu.make_async_copy(bias_s, bias_r.at[block_index(x, z, c)], self_sem.at[3])
    own_bias.start()
    own_weights[0].start()
    own_weights[1].start()
    first_own(0)
    second_own(0, 0)
    loads[0].wait()
    loads[1].wait()

    group_col, rank_col = slot_tables(len_ref, grp_ref, (slots, 1), 0)
    visible = (group_col == group_row) & (
        lax.broadcasted_iota(jnp.int32, (slots, slots), 1)
        <= lax.broadcasted_iota(jnp.int32, (slots, slots), 0)
    )

    @pl.loop(0, heads)
    def _(h):
        cols = pl.ds(pl.multiple_of(h * HD, HD), HD)
        s = lax.dot_general(q_ref[:, cols], k_ref[:, cols], NT_DIMS, preferred_element_type=jnp.float32)
        s = jnp.where(visible, s * SCALE2, NEG)
        top = jnp.max(s, axis=1, keepdims=True)
        w = jnp.where(visible, jnp.exp2(s - top), 0.0)
        own_top[h] = top
        own_sum[h] = jnp.sum(w, axis=1, keepdims=True)
        mixed[:, cols] = jnp.dot(w.astype(jnp.bfloat16), v_ref[:, cols], preferred_element_type=jnp.float32)

    def answer_back(block, k):
        tx, tz = plane_back(x, z, block)
        g, ty, tc = group_at(k)
        where = place(ty, tc, tx, tz)
        pltpu.make_async_remote_copy(
            src_ref=ans_s.at[block * GRP + g],
            dst_ref=ans_r.at[me_d * GRP + me_g],
            send_sem=a_send, recv_sem=a_recv, device_id=where, device_id_type=MESH,
        ).start()
        pltpu.make_async_remote_copy(
            src_ref=lse_s.at[block * GRP + g],
            dst_ref=lse_r.at[me_d * GRP + me_g],
            send_sem=l_send, recv_sem=l_recv, device_id=where, device_id_type=MESH,
        ).start()

    steps = 4
    span = plen // steps
    part = rows // steps

    def stage(i, parity, scoring, weighing, mixing, first=False):
        other = 1 - parity
        if scoring:
            if first:
                wait_bytes(qr.at[pl.ds(0, GRP - 1)], q_recv.at[0])
                own_query.wait()
            else:
                wait_bytes(qr.at[pl.ds(i * GRP, GRP)], q_recv.at[i])
            peak[...] = jnp.full_like(peak, NEG)
        if mixing:
            acc[...] = jnp.zeros_like(acc)

        @pl.loop(0, steps)
        def _(j):
            keys = pl.ds(pl.multiple_of(j * span, span), span)
            if scoring:
                block = qr[pl.ds(i * GRP, GRP)].reshape(rows, HD)
                s = lax.dot_general(block, pk_ref[keys, :], NT_DIMS, preferred_element_type=jnp.float32)
                s_bufs[parity][:, keys] = s
                high = s[:, :HD]
                for t in range(1, span // HD):
                    high = jnp.maximum(high, s[:, t * HD : (t + 1) * HD])
                peak[...] = jnp.maximum(peak[...], high)
            if weighing:
                some = pl.ds(pl.multiple_of(j * part, part), part)
                top = tops[other, some, :]
                total = jnp.zeros((part, HD), jnp.float32)
                for t in range(plen // HD):
                    cols = slice(t * HD, (t + 1) * HD)
                    w = jnp.exp2(s_bufs[other][some, cols] * SCALE2 - top)
                    total = total + w
                    p_bufs[other][some, cols] = w.astype(jnp.bfloat16)
                sums[other, some, :] = total
            if mixing:
                acc[...] += jnp.dot(p_bufs[parity][:, keys], pv_ref[keys, :], preferred_element_type=jnp.float32)

        if mixing:
            done = i - 2
            total = jnp.sum(sums[parity], axis=1, keepdims=True)
            answer = (acc[...] / total).astype(jnp.bfloat16).reshape(GRP, CAP, HD)
            spread = (tops[parity] + jnp.log(total) * LOG2E).reshape(GRP, CAP, HD)
            diagonal = lax.broadcasted_iota(jnp.int32, (GRP, CAP, HD), 1) == lax.broadcasted_iota(
                jnp.int32, (GRP, CAP, HD), 2
            )
            lines = jnp.sum(jnp.where(diagonal, spread, 0.0), axis=1)
            for g in range(GRP):
                ans_s[done * GRP + g] = answer[g]
                lse_s[done * GRP + g] = lines[g : g + 1]
        if scoring:
            tops[parity] = jnp.broadcast_to(jnp.max(peak[...], axis=1, keepdims=True) * SCALE2, (rows, HD))

    def send_back(done):
        for k in range(GRP):
            answer_back(done, k)

    loads[2].wait()
    loads[3].wait()
    stage(0, 0, True, False, False, first=True)
    stage(1, 1, True, True, False)
    stage(2, 0, True, True, True)
    own_answer = pltpu.make_async_copy(ans_s.at[me_g], ans_r.at[me_d * GRP + me_g], self_sem.at[1])
    own_lse = pltpu.make_async_copy(lse_s.at[me_g], lse_r.at[me_d * GRP + me_g], self_sem.at[2])
    own_answer.start()
    own_lse.start()
    for k in range(1, GRP):
        answer_back(0, k)
    stage(3, 1, True, True, True)
    send_back(1)

    def stage_pairs(first_pair, last_pair):
        @pl.loop(first_pair, last_pair)
        def _(pair):
            stage(2 * pair, 0, True, True, True)
            send_back(2 * pair - 2)
            stage(2 * pair + 1, 1, True, True, True)
            send_back(2 * pair - 1)

    stage_pairs(2, 4)
    first_direct(0)
    second_own(0, 1)
    stage_pairs(4, 6)
    second_direct(0, 0)
    first_half(0)
    stage_pairs(6, 8)
    stage(DEV, 0, False, True, True)
    send_back(DEV - 2)
    stage(DEV + 1, 1, False, False, True)
    send_back(DEV - 1)

    own_bias.wait()
    wait_bytes(bias_r.at[pl.ds(0, NC * DEV - 1)], b_recv)
    for e in range(NC * DEV // 2):
        bias_all[:, e * HD : (e + 1) * HD] = bias_r[2 * e] + bias_r[2 * e + 1]

    second_direct(0, 1)
    second_own(0, 2)
    second_own(0, 3)
    first_own(1)
    second_own(1, 0)
    second_half(0, 0)
    own_answer.wait()
    own_lse.wait()
    wait_bytes(ans_r.at[pl.ds(0, GRP * DEV - 1)], a_recv)
    wait_bytes(lse_r.at[pl.ds(0, GRP * DEV - 1)], l_recv)
    unpick = lax.broadcasted_iota(jnp.int32, (slots, rows), 1) == group_col * CAP + rank_col
    unpick = unpick.astype(jnp.float32).astype(jnp.bfloat16)
    lane = lax.broadcasted_iota(jnp.int32, (slots, HD), 1)

    @pl.loop(0, heads)
    def _(h):
        cols = pl.ds(pl.multiple_of(h * HD, HD), HD)
        far = jnp.dot(
            unpick, ans_r[pl.ds(h * GRP, GRP)].reshape(rows, HD), preferred_element_type=jnp.float32
        )
        spread = jnp.zeros((slots, HD), jnp.float32)
        for g in range(GRP):
            spread = jnp.where(group_col == g, lse_r[h * GRP + g], spread)
        far_top = jnp.sum(jnp.where(lane == rank_col, spread, 0.0), axis=1, keepdims=True)
        top = own_top[h]
        joint = jnp.maximum(far_top, top)
        far_weight = jnp.exp2(far_top - joint)
        own_weight = jnp.exp2(top - joint)
        below = far_weight + own_weight * own_sum[h]
        mixed[:, cols] = (far_weight * far + own_weight * mixed[:, cols]) / below

    second_direct(0, 2)
    second_direct(0, 3)
    first_direct(1)
    second_own(1, 1)
    second_own(1, 2)
    loads[4].wait()

    @pl.loop(0, slots // 16)
    def _(r):
        some = pl.ds(pl.multiple_of(r * 16, 16), 16)
        summed = x_ref[some, :].astype(jnp.float32) + mixed[some, :]
        tok[some, :] = norm_rows(summed, again_ref[...], ashift_ref[...]).astype(jnp.bfloat16)

    def y_copy(src, dst, send_sem, recv_sem, step):
        return pltpu.make_async_remote_copy(
            src_ref=src, dst_ref=dst, send_sem=send_sem, recv_sem=recv_sem,
            device_id=place(lax.rem(y + step + NY, NY), c, x, z), device_id_type=MESH,
        )

    def token(pos, part=None):
        return tok.at[pl.ds(pos * slots, slots)] if part is None else tok.at[
            pl.ds(pos * slots + part * (slots // 2), slots // 2)
        ]

    sent = []
    for n, (part, target, step) in enumerate(((0, 2, 1), (1, 1, -1), (1, 2, 1), (0, 1, -1))):
        sent.append(y_copy(token(0, part), token(target, part), t_send.at[n], t_recv.at[n], step))
        sent[-1].start()
    own_weights[0].wait()
    own_weights[1].wait()
    width = q_ref.shape[1]
    tile = 256
    per_tile = tile // 64

    def up(first, count):
        rows_ = pl.ds(first * slots, count * slots)

        @pl.loop(0, NC * DEV // per_tile)
        def _(n):
            cols = pl.ds(pl.multiple_of(n * tile, tile), tile)
            u = lax.dot_general(
                tok[rows_, :], wu[pl.ds(n * per_tile, per_tile)].reshape(tile, width), NT_DIMS,
                preferred_element_type=jnp.float32,
            )
            u = u + bias_all[:, cols]
            hidden[rows_, cols] = jax.nn.gelu(u, approximate=True).astype(jnp.bfloat16)

    def down(first, count, low, high):
        rows_ = pl.ds(first * slots, count * slots)

        @pl.loop(low * (width // tile // 2), high * (width // tile // 2))
        def _(n):
            cols = pl.ds(pl.multiple_of(n * tile, tile), tile)
            total_acc[rows_, cols] = jnp.dot(
                hidden[rows_, :], wd[:, :, cols].reshape(NC * DEV * 64, tile),
                preferred_element_type=jnp.float32,
            )

    second_direct(1, 0)
    first_half(1)
    second_own(1, 3)
    for k in (1, 2, 3):
        second_half(0, k)
    cross_wait(0)
    for n, (part, origin, step) in enumerate(((0, 2, 1), (1, 1, -1))):
        wait_bytes(token(origin, part), t_recv.at[n])
        sent.append(y_copy(token(origin, part), token(3, part), t_send.at[4 + n], t_recv.at[4 + n], step))
        sent[-1].start()
    second_direct(1, 1)
    second_direct(1, 2)
    up(0, 1)
    wait_bytes(token(2, 1), t_recv.at[2])
    wait_bytes(token(1, 0), t_recv.at[3])
    second_direct(1, 3)
    up(1, 2)
    wait_bytes(token(3, 0), t_recv.at[4])
    wait_bytes(token(3, 1), t_recv.at[5])
    up(3, 1)
    for k in range(4):
        second_half(1, k)
    cross_wait(1)
    cut = width // 2

    def ship(src, dst, send_sem, recv_sem, side):
        sent.append(y_copy(src, dst, send_sem, recv_sem, 1 - 2 * side))
        sent[-1].start()

    for side in range(2):
        down(3, 1, side, side + 1)
        half_s[side] = total_acc[3 * slots :, side * cut : (side + 1) * cut].astype(jnp.bfloat16)
        ship(half_s.at[side], half_r.at[side], h_send.at[side], h_recv.at[side], side)
    for rest in range(2):
        side = 1 - rest
        at = slice((1 + side) * slots, (2 + side) * slots)
        down(1, 2, rest, rest + 1)
        part_s[side, 1] = total_acc[at, rest * cut : (rest + 1) * cut].astype(jnp.bfloat16)
        ship(part_s.at[side, 1], part_r.at[side, 1], p_send.at[side, 1], p_recv.at[side, 1], side)
    for side in range(2):
        at = slice((1 + side) * slots, (2 + side) * slots)
        wait_bytes(half_r.at[side], h_recv.at[side])
        joined = total_acc[at, side * cut : (side + 1) * cut] + half_r[side].astype(jnp.float32)
        part_s[side, 0] = joined.astype(jnp.bfloat16)
        ship(part_s.at[side, 0], part_r.at[side, 0], p_send.at[side, 0], p_recv.at[side, 0], side)
    down(0, 1, 0, 2)
    for kind in (1, 0):
        for side in range(2):
            wait_bytes(part_r.at[side, kind], p_recv.at[side, kind])

    @pl.loop(0, slots // 16)
    def _(r):
        some = pl.ds(pl.multiple_of(r * 16, 16), 16)
        total = total_acc[some, :] + tok[some, :].astype(jnp.float32) + dbias_ref[...]
        low = part_r[0, 0, some, :].astype(jnp.float32) + part_r[1, 1, some, :].astype(jnp.float32)
        high = part_r[0, 1, some, :].astype(jnp.float32) + part_r[1, 0, some, :].astype(jnp.float32)
        total = total + jnp.concatenate([low, high], axis=1)
        out_ref[some, :] = norm_rows(total, ogain_ref[...], oshift_ref[...]).astype(jnp.bfloat16)

    for copy in sent:
        copy.wait_send()
    wait_bytes(qs.at[pl.ds(0, GRP * DEV - 1)], q_send)
    wait_bytes(ans_s.at[pl.ds(0, GRP * DEV - 1)], a_send)
    wait_bytes(lse_s.at[pl.ds(0, GRP * DEV - 1)], l_send)
    wait_bytes(bias_r.at[pl.ds(0, NC * DEV - 1)], b_send)
    for ab in range(2):
        wait_bytes(weights[ab].at[pl.ds(0, NC * DEV - 1)], w_send.at[ab])


def vmem():
    return pl.BlockSpec(memory_space=pltpu.VMEM)


def on_device(
    queries, keys, values, layer_input, lengths, groups, prefix_keys, prefix_values,
    up_weight, up_bias, down_weight, down_bias, attn_gain, attn_shift, out_gain, out_shift,
):
    slots, width = queries.shape
    heads = width // HD
    plen = prefix_keys.shape[1]
    rows = GRP * CAP
    local = up_bias.shape[0]
    units = NC * DEV * local
    f32, bf16 = jnp.float32, jnp.bfloat16
    dma = pltpu.SemaphoreType.DMA
    smem = pl.BlockSpec(memory_space=pltpu.SMEM)
    anywhere = pl.BlockSpec(memory_space=pl.ANY)
    messages = pltpu.VMEM((GRP * DEV, CAP, HD), bf16)
    lines = pltpu.VMEM((GRP * DEV, 1, HD), f32)
    return pl.pallas_call(
        layer_kernel,
        out_shape=jax.ShapeDtypeStruct((slots, width), bf16),
        in_specs=[smem] * 2 + [vmem()] * 2 + [anywhere] * 7 + [vmem()] * 5,
        out_specs=vmem(),
        scratch_shapes=[
            pltpu.VMEM((slots, width), bf16),
            pltpu.VMEM((slots, width), bf16),
            pltpu.VMEM((slots, width), bf16),
            pltpu.VMEM((plen, HD), bf16),
            pltpu.VMEM((plen, HD), bf16),
            messages, messages, messages, messages, lines, lines,
            pltpu.VMEM((1, HD), f32),
            pltpu.VMEM((NC * DEV, 1, HD), f32),
            pltpu.VMEM((1, units), f32),
            pltpu.VMEM((rows, plen), f32),
            pltpu.VMEM((rows, plen), f32),
            pltpu.VMEM((rows, plen), bf16),
            pltpu.VMEM((rows, plen), bf16),
            pltpu.VMEM((rows, HD), f32),
            pltpu.VMEM((rows, HD), f32),
            pltpu.VMEM((2, rows, HD), f32),
            pltpu.VMEM((2, rows, HD), f32),
            pltpu.VMEM((slots, width), f32),
            pltpu.VMEM((heads, slots, 1), f32),
            pltpu.VMEM((heads, slots, 1), f32),
            pltpu.VMEM((NC * DEV, local, width), bf16),
            pltpu.VMEM((NC * DEV, local, width), bf16),
            pltpu.VMEM((NY * slots, width), bf16),
            pltpu.VMEM((NY * slots, units), bf16),
            pltpu.VMEM((NY * slots, width), f32),
            pltpu.VMEM((2, slots, width // 2), bf16),
            pltpu.VMEM((2, slots, width // 2), bf16),
            pltpu.VMEM((2, 2, slots, width // 2), bf16),
            pltpu.VMEM((2, 2, slots, width // 2), bf16),
            dma, dma((DEV,)), dma, dma, dma, dma, dma, dma, dma((4,)), dma((7,)),
            dma((2,)), dma((4, 5, 4)), dma((2,)), dma((6,)), dma((6,)), dma((2,)), dma((2,)), dma((2, 2)), dma((2, 2)),
        ],
        compiler_params=pltpu.CompilerParams(collective_id=0, has_side_effects=True, vmem_limit_bytes=LIMIT),
        name="layer",
    )(
        lengths, groups, queries, up_bias[None], keys, values, layer_input,
        prefix_keys[0], prefix_values[0], up_weight.T, down_weight,
        attn_gain[None], attn_shift[None], down_bias[None], out_gain[None], out_shift[None],
    )


def solution(mesh):
    fine = Mesh(mesh.devices.reshape(NY, NC, NX, NZ), ("y", "c", "x", "z"))
    grp, dev = ("y", "c"), ("x", "z")
    every = grp + dev
    token_rows = P(every, None)
    placed = (
        (token_rows,) * 6
        + (P(grp, None, dev),) * 2
        + (P(None, every), P(every), P(every, None))
        + (P(),) * 5
    )
    return jax.shard_map(on_device, mesh=fine, in_specs=placed, out_specs=token_rows, check_vma=False)
```

```python
import functools

import jax
import jax.numpy as jnp
from jax import lax
from jax.experimental import pallas as pl
from jax.experimental.pallas import tpu as pltpu
from jax.sharding import Mesh, PartitionSpec as P

HD = 128
NY, NC, NX, NZ = 4, 2, 4, 4
GRP, DEV = NY * NC, NX * NZ
CAP = 32
LOG2E = 1.4426950408889634
SCALE2 = HD**-0.5 * LOG2E
NORM_EPS = 1e-12
NEG = -1e30
MESH = pl.DeviceIdType.MESH
NT_DIMS = (((1,), (1,)), ((), ()))
LIMIT = 64 * 1024 * 1024 - 65536


def coordinates():
    return tuple(lax.axis_index(name) for name in ("y", "c", "x", "z"))


def place(y, c, x, z):
    return {"y": y, "c": c, "x": x, "z": z}


def plane_at(x, z, block):
    return lax.rem(x + block // NZ, NX), lax.rem(z + lax.rem(block, NZ), NZ)


def plane_back(x, z, block):
    return lax.rem(x + NX - block // NZ, NX), lax.rem(z + NZ - lax.rem(block, NZ), NZ)


def block_index(x, z, c):
    return z * (NC * NX) + c * NX + x


def wait_bytes(ref, sem):
    pltpu.make_async_copy(ref, ref, sem).wait()


def norm_rows(summed, gain, shift):
    mean = jnp.mean(summed, axis=-1, keepdims=True)
    centred = summed - mean
    spread = jnp.mean(centred * centred, axis=-1, keepdims=True)
    return centred * lax.rsqrt(spread + NORM_EPS) * gain + shift


def slot_tables(len_ref, grp_ref, shape, dim):
    slot = lax.broadcasted_iota(jnp.int32, shape, dim)
    start = jnp.int32(0)
    group = jnp.zeros(shape, jnp.int32)
    rank = jnp.zeros(shape, jnp.int32)
    for request in range(len_ref.shape[1]):
        length = len_ref[0, request]
        inside = (slot >= start) & (slot < start + length)
        group = jnp.where(inside, grp_ref[0, request], group)
        rank = jnp.where(inside, slot - start, rank)
        start = start + length
    return group, rank


def layer_kernel(
    len_ref, grp_ref, q_ref, bias_ref, k_in, v_in, x_in, pk_in, pv_in, up_in, down_in,
    again_ref, ashift_ref, dbias_ref, ogain_ref, oshift_ref,
    out_ref,
    k_ref, v_ref, x_ref, pk_ref, pv_ref,
    qs, qr, ans_s, ans_r, lse_s, lse_r, bias_s, bias_r, bias_all,
    s0, s1, p0, p1, acc, peak, tops, sums, mixed, own_top, own_sum,
    wu, wd, tok, hidden, total_acc, half_s, half_r, part_s, part_r,
    q_send, q_recv, a_send, a_recv, l_send, l_recv, b_send, b_recv, self_sem, in_sem,
    w_send, w_recv, w_cross, t_send, t_recv, h_send, h_recv, p_send, p_recv,
):
    y, c, x, z = coordinates()
    me_g = y * NC + c
    me_d = x * NZ + z
    slots = q_ref.shape[0]
    heads = q_ref.shape[1] // HD
    s_bufs, p_bufs = (s0, s1), (p0, p1)
    rows = GRP * CAP
    plen = pk_ref.shape[0]

    def group_at(k):
        g = lax.rem(me_g + k, GRP)
        return g, g // NC, lax.rem(g, NC)

    loads = [
        pltpu.make_async_copy(src, dst, in_sem.at[n])
        for n, (src, dst) in enumerate(
            ((k_in, k_ref), (v_in, v_ref), (pk_in, pk_ref), (pv_in, pv_ref), (x_in, x_ref))
        )
    ]
    for load in loads:
        load.start()
    barrier = pltpu.get_barrier_semaphore()

    def greet(block, k):
        tx, tz = plane_at(x, z, block)
        _, ty, tc = group_at(k)
        pl.semaphore_signal(barrier, inc=1, device_id=place(ty, tc, tx, tz), device_id_type=MESH)

    for k in range(1, GRP):
        greet(0, k)

    @pl.loop(1, DEV)
    def _(block):
        for k in range(GRP):
            greet(block, k)

    group_row, rank_row = slot_tables(len_ref, grp_ref, (1, slots), 1)
    pick = lax.broadcasted_iota(jnp.int32, (rows, slots), 0) == group_row * CAP + rank_row
    pick = pick.astype(jnp.float32).astype(jnp.bfloat16)
    line = bias_ref[...].astype(jnp.float32)
    line = jnp.concatenate([line, line], axis=1)
    side = lax.broadcasted_iota(jnp.int32, line.shape, 1) // (HD // 2)
    bias_s[...] = jnp.where(side == lax.rem(x, 2), line, 0.0)
    for d in range(heads):
        packed = jnp.dot(pick, q_ref[:, d * HD : (d + 1) * HD], preferred_element_type=jnp.float32)
        packed = packed.astype(jnp.bfloat16).reshape(GRP, CAP, HD)
        for g in range(GRP):
            qs[g * DEV + d] = packed[g]
    pl.semaphore_wait(barrier, GRP * DEV - 1)

    weights = (wu, wd)
    sources = (up_in, down_in)
    ring_steps = (0, -1, 1, 2)
    strip = up_in.shape[0] // 2

    def block_of(q, r1, r2):
        rx, rz = (r1, r2) if q % 2 == 0 else (r2, r1)
        return block_index(lax.rem(x + rx + NX, NX), lax.rem(z + rz + NZ, NZ), c)

    def along(q, axis, step):
        if (q + axis) % 2 == 0:
            return place(y, c, lax.rem(x + step + NX, NX), z)
        return place(y, c, x, lax.rem(z + step + NZ, NZ))

    partner = place(y, 1 - c, x, z)

    def strip_of(block, q, part):
        first = (q % 2) * strip
        if part is None:
            return block.at[pl.ds(first, strip)]
        return block.at[pl.ds(first + part * (strip // 2), strip // 2)]

    def weight_refs(q, r1, r2, part):
        dst = strip_of(weights[q // 2].at[block_of(q, r1, r2)], q, part)
        src = strip_of(sources[q // 2], q, part) if (r1 == 0 and r2 == 0) else dst
        return src, dst

    def weight_send(q, r1, r2, part, axis, step, phase, kind):
        src, dst = weight_refs(q, r1, r2, part)
        pltpu.make_async_remote_copy(
            src_ref=src, dst_ref=dst, send_sem=w_send.at[q // 2], recv_sem=w_recv.at[q, phase, kind],
            device_id=along(q, axis, step), device_id_type=MESH,
        ).start()

    def weight_cross(q, r1, r2):
        src, dst = weight_refs(q, r1, r2, None)
        pltpu.make_async_remote_copy(
            src_ref=src, dst_ref=dst, send_sem=w_send.at[q // 2], recv_sem=w_cross.at[q // 2],
            device_id=partner, device_id_type=MESH,
        ).start()

    def weight_wait(q, phase, kind):
        size = strip if kind < 2 else strip // 2
        wait_bytes(weights[q // 2].at[0, pl.ds(0, size)], w_recv.at[q, phase, kind])

    def both(tensor):
        return (2 * tensor, 2 * tensor + 1)

    def first_own(tensor):
        for q in both(tensor):
            weight_send(q, 0, 0, None, 0, 1, 0, 0)
            weight_send(q, 0, 0, None, 0, -1, 0, 1)
            weight_cross(q, 0, 0)

    def first_direct(tensor):
        for q in both(tensor):
            weight_wait(q, 0, 0)
            weight_send(q, -1, 0, 0, 0, 1, 0, 2)
            weight_wait(q, 0, 1)
            weight_send(q, 1, 0, 1, 0, -1, 0, 3)
            weight_cross(q, -1, 0)
            weight_cross(q, 1, 0)

    def first_half(tensor):
        for q in both(tensor):
            weight_wait(q, 0, 2)
            weight_wait(q, 0, 3)
            weight_cross(q, 2, 0)

    def second_own(tensor, k):
        for q in both(tensor):
            weight_send(q, ring_steps[k], 0, None, 1, 1, 1 + k, 0)
            weight_send(q, ring_steps[k], 0, None, 1, -1, 1 + k, 1)

    def second_direct(tensor, k):
        r1 = ring_steps[k]
        for q in both(tensor):
            weight_wait(q, 1 + k, 0)
            weight_send(q, r1, -1, 0, 1, 1, 1 + k, 2)
            weight_wait(q, 1 + k, 1)
            weight_send(q, r1, 1, 1, 1, -1, 1 + k, 3)
            weight_cross(q, r1, -1)
            weight_cross(q, r1, 1)

    def second_half(tensor, k):
        for q in both(tensor):
            weight_wait(q, 1 + k, 2)
            weight_wait(q, 1 + k, 3)
            weight_cross(q, ring_steps[k], 2)

    def cross_wait(tensor):
        wait_bytes(weights[tensor].at[pl.ds(0, DEV)], w_cross.at[tensor])

    own_weights = [
        pltpu.make_async_copy(sources[ab], weights[ab].at[block_index(x, z, c)], in_sem.at[5 + ab])
        for ab in range(2)
    ]

    def send_query(block, k):
        tx, tz = plane_at(x, z, block)
        g, ty, tc = group_at(k)
        pltpu.make_async_remote_copy(
            src_ref=qs.at[g * DEV + tx * NZ + tz],
            dst_ref=qr.at[block * GRP + me_g],
            send_sem=q_send,
            recv_sem=q_recv.at[block],
            device_id=place(ty, tc, tx, tz),
            device_id_type=MESH,
        ).start()

    own_query = pltpu.make_async_copy(qs.at[me_g * DEV + me_d], qr.at[me_g], self_sem.at[0])
    own_query.start()
    for k in range(1, GRP):
        send_query(0, k)

    @pl.loop(1, DEV)
    def _(block):
        for k in range(GRP):
            send_query(block, k)

    for k in range(1, NC * DEV):
        tc = lax.rem(c + k // DEV, NC)
        tx, tz = plane_at(x, z, k % DEV)
        pltpu.make_async_remote_copy(
            src_ref=bias_s,
            dst_ref=bias_r.at[block_index(x, z, c)],
            send_sem=b_send,
            recv_sem=b_recv,
            device_id=place(y, tc, tx, tz),
            device_id_type=MESH,
        ).start()
    own_bias = pltpu.make_async_copy(bias_s, bias_r.at[block_index(x, z, c)], self_sem.at[3])
    own_bias.start()
    own_weights[0].start()
    own_weights[1].start()
    first_own(0)
    second_own(0, 0)
    loads[0].wait()
    loads[1].wait()

    group_col, rank_col = slot_tables(len_ref, grp_ref, (slots, 1), 0)
    visible = (group_col == group_row) & (
        lax.broadcasted_iota(jnp.int32, (slots, slots), 1)
        <= lax.broadcasted_iota(jnp.int32, (slots, slots), 0)
    )

    @pl.loop(0, heads)
    def _(h):
        cols = pl.ds(pl.multiple_of(h * HD, HD), HD)
        s = lax.dot_general(q_ref[:, cols], k_ref[:, cols], NT_DIMS, preferred_element_type=jnp.float32)
        s = jnp.where(visible, s * SCALE2, NEG)
        top = jnp.max(s, axis=1, keepdims=True)
        w = jnp.where(visible, jnp.exp2(s - top), 0.0)
        own_top[h] = top
        own_sum[h] = jnp.sum(w, axis=1, keepdims=True)
        mixed[:, cols] = jnp.dot(w.astype(jnp.bfloat16), v_ref[:, cols], preferred_element_type=jnp.float32)

    def answer_back(block, k):
        tx, tz = plane_back(x, z, block)
        g, ty, tc = group_at(k)
        where = place(ty, tc, tx, tz)
        pltpu.make_async_remote_copy(
            src_ref=ans_s.at[block * GRP + g],
            dst_ref=ans_r.at[me_d * GRP + me_g],
            send_sem=a_send, recv_sem=a_recv, device_id=where, device_id_type=MESH,
        ).start()
        pltpu.make_async_remote_copy(
            src_ref=lse_s.at[block * GRP + g],
            dst_ref=lse_r.at[me_d * GRP + me_g],
            send_sem=l_send, recv_sem=l_recv, device_id=where, device_id_type=MESH,
        ).start()

    steps = 4
    span = plen // steps
    part = rows // steps

    def stage(i, parity, scoring, weighing, mixing, first=False):
        other = 1 - parity
        if scoring:
            if first:
                wait_bytes(qr.at[pl.ds(0, GRP - 1)], q_recv.at[0])
                own_query.wait()
            else:
                wait_bytes(qr.at[pl.ds(i * GRP, GRP)], q_recv.at[i])
            peak[...] = jnp.full_like(peak, NEG)
        if mixing:
            acc[...] = jnp.zeros_like(acc)

        @pl.loop(0, steps)
        def _(j):
            keys = pl.ds(pl.multiple_of(j * span, span), span)
            if scoring:
                block = qr[pl.ds(i * GRP, GRP)].reshape(rows, HD)
                s = lax.dot_general(block, pk_ref[keys, :], NT_DIMS, preferred_element_type=jnp.float32)
                s_bufs[parity][:, keys] = s
                high = s[:, :HD]
                for t in range(1, span // HD):
                    high = jnp.maximum(high, s[:, t * HD : (t + 1) * HD])
                peak[...] = jnp.maximum(peak[...], high)
            if weighing:
                some = pl.ds(pl.multiple_of(j * part, part), part)
                top = tops[other, some, :]
                total = jnp.zeros((part, HD), jnp.float32)
                for t in range(plen // HD):
                    cols = slice(t * HD, (t + 1) * HD)
                    w = jnp.exp2(s_bufs[other][some, cols] * SCALE2 - top)
                    total = total + w
                    p_bufs[other][some, cols] = w.astype(jnp.bfloat16)
                sums[other, some, :] = total
            if mixing:
                acc[...] += jnp.dot(p_bufs[parity][:, keys], pv_ref[keys, :], preferred_element_type=jnp.float32)

        if mixing:
            done = i - 2
            total = jnp.sum(sums[parity], axis=1, keepdims=True)
            answer = (acc[...] / total).astype(jnp.bfloat16).reshape(GRP, CAP, HD)
            spread = (tops[parity] + jnp.log(total) * LOG2E).reshape(GRP, CAP, HD)
            diagonal = lax.broadcasted_iota(jnp.int32, (GRP, CAP, HD), 1) == lax.broadcasted_iota(
                jnp.int32, (GRP, CAP, HD), 2
            )
            lines = jnp.sum(jnp.where(diagonal, spread, 0.0), axis=1)
            for g in range(GRP):
                ans_s[done * GRP + g] = answer[g]
                lse_s[done * GRP + g] = lines[g : g + 1]
        if scoring:
            tops[parity] = jnp.broadcast_to(jnp.max(peak[...], axis=1, keepdims=True) * SCALE2, (rows, HD))

    def send_back(done):
        for k in range(GRP):
            answer_back(done, k)

    loads[2].wait()
    loads[3].wait()
    stage(0, 0, True, False, False, first=True)
    stage(1, 1, True, True, False)
    stage(2, 0, True, True, True)
    own_answer = pltpu.make_async_copy(ans_s.at[me_g], ans_r.at[me_d * GRP + me_g], self_sem.at[1])
    own_lse = pltpu.make_async_copy(lse_s.at[me_g], lse_r.at[me_d * GRP + me_g], self_sem.at[2])
    own_answer.start()
    own_lse.start()
    for k in range(1, GRP):
        answer_back(0, k)
    stage(3, 1, True, True, True)
    send_back(1)

    def stage_pairs(first_pair, last_pair):
        @pl.loop(first_pair, last_pair)
        def _(pair):
            stage(2 * pair, 0, True, True, True)
            send_back(2 * pair - 2)
            stage(2 * pair + 1, 1, True, True, True)
            send_back(2 * pair - 1)

    stage_pairs(2, 3)
    first_direct(0)
    second_own(0, 1)
    stage_pairs(3, 5)
    second_direct(0, 0)
    first_half(0)
    second_own(0, 2)
    stage_pairs(5, 8)
    stage(DEV, 0, False, True, True)
    send_back(DEV - 2)
    stage(DEV + 1, 1, False, False, True)
    send_back(DEV - 1)

    own_bias.wait()
    wait_bytes(bias_r.at[pl.ds(0, NC * DEV - 1)], b_recv)
    for e in range(NC * DEV // 2):
        bias_all[:, e * HD : (e + 1) * HD] = bias_r[2 * e] + bias_r[2 * e + 1]

    second_direct(0, 1)
    second_direct(0, 2)
    second_own(0, 3)
    first_own(1)
    second_own(1, 0)
    second_half(0, 0)
    own_answer.wait()
    own_lse.wait()
    wait_bytes(ans_r.at[pl.ds(0, GRP * DEV - 1)], a_recv)
    wait_bytes(lse_r.at[pl.ds(0, GRP * DEV - 1)], l_recv)
    unpick = lax.broadcasted_iota(jnp.int32, (slots, rows), 1) == group_col * CAP + rank_col
    unpick = unpick.astype(jnp.float32).astype(jnp.bfloat16)
    lane = lax.broadcasted_iota(jnp.int32, (slots, HD), 1)

    @pl.loop(0, heads)
    def _(h):
        cols = pl.ds(pl.multiple_of(h * HD, HD), HD)
        far = jnp.dot(
            unpick, ans_r[pl.ds(h * GRP, GRP)].reshape(rows, HD), preferred_element_type=jnp.float32
        )
        spread = jnp.zeros((slots, HD), jnp.float32)
        for g in range(GRP):
            spread = jnp.where(group_col == g, lse_r[h * GRP + g], spread)
        far_top = jnp.sum(jnp.where(lane == rank_col, spread, 0.0), axis=1, keepdims=True)
        top = own_top[h]
        joint = jnp.maximum(far_top, top)
        far_weight = jnp.exp2(far_top - joint)
        own_weight = jnp.exp2(top - joint)
        below = far_weight + own_weight * own_sum[h]
        mixed[:, cols] = (far_weight * far + own_weight * mixed[:, cols]) / below

    second_direct(0, 3)
    first_direct(1)
    second_own(1, 1)
    second_own(1, 2)
    loads[4].wait()

    @pl.loop(0, slots // 16)
    def _(r):
        some = pl.ds(pl.multiple_of(r * 16, 16), 16)
        summed = x_ref[some, :].astype(jnp.float32) + mixed[some, :]
        tok[some, :] = norm_rows(summed, again_ref[...], ashift_ref[...]).astype(jnp.bfloat16)

    def y_copy(src, dst, send_sem, recv_sem, step):
        return pltpu.make_async_remote_copy(
            src_ref=src, dst_ref=dst, send_sem=send_sem, recv_sem=recv_sem,
            device_id=place(lax.rem(y + step + NY, NY), c, x, z), device_id_type=MESH,
        )

    def token(pos, part=None):
        return tok.at[pl.ds(pos * slots, slots)] if part is None else tok.at[
            pl.ds(pos * slots + part * (slots // 2), slots // 2)
        ]

    sent = []
    for n, (part, target, step) in enumerate(((0, 2, 1), (1, 1, -1), (1, 2, 1), (0, 1, -1))):
        sent.append(y_copy(token(0, part), token(target, part), t_send.at[n], t_recv.at[n], step))
        sent[-1].start()
    own_weights[0].wait()
    own_weights[1].wait()
    width = q_ref.shape[1]
    tile = 256
    per_tile = tile // 64

    def up(first, count):
        rows_ = pl.ds(first * slots, count * slots)

        @pl.loop(0, NC * DEV // per_tile)
        def _(n):
            cols = pl.ds(pl.multiple_of(n * tile, tile), tile)
            u = lax.dot_general(
                tok[rows_, :], wu[pl.ds(n * per_tile, per_tile)].reshape(tile, width), NT_DIMS,
                preferred_element_type=jnp.float32,
            )
            u = u + bias_all[:, cols]
            hidden[rows_, cols] = jax.nn.gelu(u, approximate=True).astype(jnp.bfloat16)

    def down(first, count, low, high):
        rows_ = pl.ds(first * slots, count * slots)

        @pl.loop(low * (width // tile // 2), high * (width // tile // 2))
        def _(n):
            cols = pl.ds(pl.multiple_of(n * tile, tile), tile)
            total_acc[rows_, cols] = jnp.dot(
                hidden[rows_, :], wd[:, :, cols].reshape(NC * DEV * 64, tile),
                preferred_element_type=jnp.float32,
            )

    second_direct(1, 0)
    first_half(1)
    second_own(1, 3)
    for k in (1, 2, 3):
        second_half(0, k)
    cross_wait(0)
    for n, (part, origin, step) in enumerate(((0, 2, 1), (1, 1, -1))):
        wait_bytes(token(origin, part), t_recv.at[n])
        sent.append(y_copy(token(origin, part), token(3, part), t_send.at[4 + n], t_recv.at[4 + n], step))
        sent[-1].start()
    second_direct(1, 1)
    second_direct(1, 2)
    up(0, 1)
    wait_bytes(token(2, 1), t_recv.at[2])
    wait_bytes(token(1, 0), t_recv.at[3])
    second_direct(1, 3)
    up(1, 2)
    wait_bytes(token(3, 0), t_recv.at[4])
    wait_bytes(token(3, 1), t_recv.at[5])
    up(3, 1)
    for k in range(4):
        second_half(1, k)
    cross_wait(1)
    cut = width // 2

    def ship(src, dst, send_sem, recv_sem, side):
        sent.append(y_copy(src, dst, send_sem, recv_sem, 1 - 2 * side))
        sent[-1].start()

    for side in range(2):
        down(3, 1, side, side + 1)
        half_s[side] = total_acc[3 * slots :, side * cut : (side + 1) * cut].astype(jnp.bfloat16)
        ship(half_s.at[side], half_r.at[side], h_send.at[side], h_recv.at[side], side)
    for rest in range(2):
        side = 1 - rest
        at = slice((1 + side) * slots, (2 + side) * slots)
        down(1, 2, rest, rest + 1)
        part_s[side, 1] = total_acc[at, rest * cut : (rest + 1) * cut].astype(jnp.bfloat16)
        ship(part_s.at[side, 1], part_r.at[side, 1], p_send.at[side, 1], p_recv.at[side, 1], side)
    for side in range(2):
        at = slice((1 + side) * slots, (2 + side) * slots)
        wait_bytes(half_r.at[side], h_recv.at[side])
        joined = total_acc[at, side * cut : (side + 1) * cut] + half_r[side].astype(jnp.float32)
        part_s[side, 0] = joined.astype(jnp.bfloat16)
        ship(part_s.at[side, 0], part_r.at[side, 0], p_send.at[side, 0], p_recv.at[side, 0], side)
    down(0, 1, 0, 2)
    for kind in (1, 0):
        for side in range(2):
            wait_bytes(part_r.at[side, kind], p_recv.at[side, kind])

    @pl.loop(0, slots // 16)
    def _(r):
        some = pl.ds(pl.multiple_of(r * 16, 16), 16)
        total = total_acc[some, :] + tok[some, :].astype(jnp.float32) + dbias_ref[...]
        low = part_r[0, 0, some, :].astype(jnp.float32) + part_r[1, 1, some, :].astype(jnp.float32)
        high = part_r[0, 1, some, :].astype(jnp.float32) + part_r[1, 0, some, :].astype(jnp.float32)
        total = total + jnp.concatenate([low, high], axis=1)
        out_ref[some, :] = norm_rows(total, ogain_ref[...], oshift_ref[...]).astype(jnp.bfloat16)

    for copy in sent:
        copy.wait_send()
    wait_bytes(qs.at[pl.ds(0, GRP * DEV - 1)], q_send)
    wait_bytes(ans_s.at[pl.ds(0, GRP * DEV - 1)], a_send)
    wait_bytes(lse_s.at[pl.ds(0, GRP * DEV - 1)], l_send)
    wait_bytes(bias_r.at[pl.ds(0, NC * DEV - 1)], b_send)
    for ab in range(2):
        wait_bytes(weights[ab].at[pl.ds(0, NC * DEV - 1)], w_send.at[ab])


def vmem():
    return pl.BlockSpec(memory_space=pltpu.VMEM)


def on_device(
    queries, keys, values, layer_input, lengths, groups, prefix_keys, prefix_values,
    up_weight, up_bias, down_weight, down_bias, attn_gain, attn_shift, out_gain, out_shift,
):
    slots, width = queries.shape
    heads = width // HD
    plen = prefix_keys.shape[1]
    rows = GRP * CAP
    local = up_bias.shape[0]
    units = NC * DEV * local
    f32, bf16 = jnp.float32, jnp.bfloat16
    dma = pltpu.SemaphoreType.DMA
    smem = pl.BlockSpec(memory_space=pltpu.SMEM)
    anywhere = pl.BlockSpec(memory_space=pl.ANY)
    messages = pltpu.VMEM((GRP * DEV, CAP, HD), bf16)
    lines = pltpu.VMEM((GRP * DEV, 1, HD), f32)
    return pl.pallas_call(
        layer_kernel,
        out_shape=jax.ShapeDtypeStruct((slots, width), bf16),
        in_specs=[smem] * 2 + [vmem()] * 2 + [anywhere] * 7 + [vmem()] * 5,
        out_specs=vmem(),
        scratch_shapes=[
            pltpu.VMEM((slots, width), bf16),
            pltpu.VMEM((slots, width), bf16),
            pltpu.VMEM((slots, width), bf16),
            pltpu.VMEM((plen, HD), bf16),
            pltpu.VMEM((plen, HD), bf16),
            messages, messages, messages, messages, lines, lines,
            pltpu.VMEM((1, HD), f32),
            pltpu.VMEM((NC * DEV, 1, HD), f32),
            pltpu.VMEM((1, units), f32),
            pltpu.VMEM((rows, plen), f32),
            pltpu.VMEM((rows, plen), f32),
            pltpu.VMEM((rows, plen), bf16),
            pltpu.VMEM((rows, plen), bf16),
            pltpu.VMEM((rows, HD), f32),
            pltpu.VMEM((rows, HD), f32),
            pltpu.VMEM((2, rows, HD), f32),
            pltpu.VMEM((2, rows, HD), f32),
            pltpu.VMEM((slots, width), f32),
            pltpu.VMEM((heads, slots, 1), f32),
            pltpu.VMEM((heads, slots, 1), f32),
            pltpu.VMEM((NC * DEV, local, width), bf16),
            pltpu.VMEM((NC * DEV, local, width), bf16),
            pltpu.VMEM((NY * slots, width), bf16),
            pltpu.VMEM((NY * slots, units), bf16),
            pltpu.VMEM((NY * slots, width), f32),
            pltpu.VMEM((2, slots, width // 2), bf16),
            pltpu.VMEM((2, slots, width // 2), bf16),
            pltpu.VMEM((2, 2, slots, width // 2), bf16),
            pltpu.VMEM((2, 2, slots, width // 2), bf16),
            dma, dma((DEV,)), dma, dma, dma, dma, dma, dma, dma((4,)), dma((7,)),
            dma((2,)), dma((4, 5, 4)), dma((2,)), dma((6,)), dma((6,)), dma((2,)), dma((2,)), dma((2, 2)), dma((2, 2)),
        ],
        compiler_params=pltpu.CompilerParams(collective_id=0, has_side_effects=True, vmem_limit_bytes=LIMIT),
        name="layer",
    )(
        lengths, groups, queries, up_bias[None], keys, values, layer_input,
        prefix_keys[0], prefix_values[0], up_weight.T, down_weight,
        attn_gain[None], attn_shift[None], down_bias[None], out_gain[None], out_shift[None],
    )


def solution(mesh):
    fine = Mesh(mesh.devices.reshape(NY, NC, NX, NZ), ("y", "c", "x", "z"))
    grp, dev = ("y", "c"), ("x", "z")
    every = grp + dev
    token_rows = P(every, None)
    placed = (
        (token_rows,) * 6
        + (P(grp, None, dev),) * 2
        + (P(None, every), P(every), P(every, None))
        + (P(),) * 5
    )
    return jax.shard_map(on_device, mesh=fine, in_specs=placed, out_specs=token_rows, check_vma=False)
```
